32 devices in a mesh: grp: 8 (over z, y), tp: 2 (over core), fs: 2 (over x).
Axes of the slice: x: 2, y: 2, z: 4, core: 2. Of those that a mesh axis runs over, the one named last changes fastest.
Arguments:
- tokens: bfloat16 [512, 4, 8192], P('grp', None, ('tp', 'fs')), may hold values from -64 to 64
- norm_gain: bfloat16 [8192], P(('tp', 'fs')), may hold values from 0.25 to 1.75
- queries: bfloat16 [512, 4, 8192], P('grp', None, ('tp', 'fs')), may hold values from -64 to 64
- rotated_key_cache: bfloat16 [512, 32, 1024], P('grp', None, ('tp', 'fs')), may hold values from -6 to 6
- head_value_cache: bfloat16 [512, 32, 1024], P('grp', None, ('tp', 'fs')), may hold values from -6 to 6
- lengths: int32 [512], P('grp'), may hold values from 2 to 32
- master: float32 [8192, 2048], P('grp', ('tp', 'fs')), may hold values from -0.0625 to 0.0625
- moment_first: float32 [8192, 2048], P('grp', ('tp', 'fs')), may hold values from -4 to 4
- moment_second: float32 [8192, 2048], P('grp', ('tp', 'fs')), may hold values from 0.1 to 1
- gradient: float32 [8192, 2048], P('grp', ('tp', 'fs')), may hold values from -6 to 6
Outputs:
- attended: bfloat16 [512, 4, 8192], P('grp', None, ('tp', 'fs'))
- appended: bfloat16 [512, 4, 2048], P('grp', None, ('tp', 'fs'))
- new_master: float32 [8192, 2048], P('grp', ('tp', 'fs'))
- new_first: float32 [8192, 2048], P('grp', ('tp', 'fs'))
- new_second: float32 [8192, 2048], P('grp', ('tp', 'fs'))
The draws below stay inside these ranges and needn't reach their ends.
All inputs are finite; a program needn't handle non-finite values.
Results may differ from the reference program's by a relative error of at most 0.0057.
Values may be sent and summed in bfloat16 or wider, within the bound.
A program may use at most 128 MiB of HBM per device.

```python
import math
import jax
import jax.numpy as jnp
from jax import lax

MODEL_WIDTH = 8192
QUERY_HEADS = 64
KEY_VALUE_HEADS = 8
HEAD_SIZE = 128
REPLICA_ROWS = 64
CACHE_SLOTS = 32
NEW_TOKENS = 4
TOTAL_ROWS = 512
KV_COLS = 2048
N_GRP = 8


def drawn_draw(key):
    cache_seed = jax.random.fold_in(key, 7001)
    query_seed = jax.random.fold_in(key, 7002)
    cache_dimensions = (TOTAL_ROWS, CACHE_SLOTS, KEY_VALUE_HEADS * HEAD_SIZE)
    query_shape = (TOTAL_ROWS, NEW_TOKENS, QUERY_HEADS * HEAD_SIZE)
    cache_key_seeds = jnp.clip(jax.random.normal(cache_seed, cache_dimensions, jnp.float32), -6.0, 6.0)
    query_draw = jnp.clip(jax.random.normal(query_seed, query_shape, jnp.float32), -6.0, 6.0)
    return (cache_key_seeds, query_draw)


def draw_rotated_key_cache(key, part):
    return drawn_draw(key)[0].astype(jnp.bfloat16)


def draw_queries(key, part):
    return drawn_draw(key)[1].astype(jnp.bfloat16)


def draw_tokens(key, part):
    base_seed = jax.random.fold_in(key, 8001)
    shape = (TOTAL_ROWS, NEW_TOKENS, MODEL_WIDTH)
    values = jnp.clip(jax.random.normal(base_seed, shape, jnp.float32), -6.0, 6.0)
    return values.astype(jnp.bfloat16)


def place_ends(result, stream_key, low, high):
    longest = result.shape.index(max(result.shape))
    spots = []
    for shift in (0, 1):
        where = [jax.random.randint(jax.random.fold_in(stream_key, axis), (), 0, length) for axis, length in enumerate(result.shape)]
        where[longest] = (where[longest] + shift) % result.shape[longest]
        spots.append(tuple(where))
    return result.at[spots[0]].set(low).at[spots[1]].set(high)


def block_levels(stream_key, shape, cuts, low, largest):
    def one(axis_at, blocks):
        steps = jax.random.uniform(jax.random.fold_in(jax.random.fold_in(stream_key, 6), axis_at), (blocks,), jnp.float32, low / len(cuts), largest / len(cuts))
        return jnp.repeat(jnp.exp(steps), shape[axis_at] // blocks).reshape((-1,) + (1,) * (len(shape) - axis_at - 1))

    factor_of = one(*cuts[0])
    for cut in cuts[1:]:
        factor_of = factor_of * one(*cut)
    return factor_of


def noise(key, shape, scale, limit, cuts=(), held_as=jnp.bfloat16):
    factor_of = block_levels(key, shape, cuts, -0.22, 0.18) if cuts else 1.0
    result = jax.random.normal(key, shape, jnp.float32) * scale * factor_of
    return jnp.minimum(jnp.maximum(result, -limit), limit).astype(held_as)


def setup_inputs(seed: int = 0) -> dict:
    splits = jax.random.split(jax.random.key(seed), 11)
    return {
        "tokens": draw_tokens(jax.random.fold_in(splits[10], 71), 0),
        "norm_gain": jnp.clip(1.0 + 0.15 * jax.random.normal(splits[1], (MODEL_WIDTH,), jnp.float32), 0.25, 1.75).astype(jnp.bfloat16),
        "queries": draw_queries(jax.random.fold_in(splits[10], 71), 0),
        "rotated_key_cache": draw_rotated_key_cache(jax.random.fold_in(splits[10], 71), 0),
        "head_value_cache": noise(splits[4], (TOTAL_ROWS, CACHE_SLOTS, KEY_VALUE_HEADS * HEAD_SIZE), 1.0, 6.0, ((0, 8), (2, 4))),
        "lengths": place_ends(jax.random.randint(splits[5], (TOTAL_ROWS,), 2, CACHE_SLOTS + 1), jax.random.fold_in(splits[5], 1), 2, CACHE_SLOTS).astype(jnp.int32),
        "master": noise(splits[6], (MODEL_WIDTH, KV_COLS), MODEL_WIDTH ** -0.5, 0.0625, ((0, 8), (1, 4)), jnp.float32),
        "moment_first": noise(splits[7], (MODEL_WIDTH, KV_COLS), 0.3, 4.0, ((0, 8), (1, 4)), jnp.float32),
        "moment_second": jnp.clip(jnp.exp(math.log(1.0) - 2.3025851 * jax.random.uniform(splits[8], (MODEL_WIDTH, KV_COLS), jnp.float32) ** block_levels(splits[8], (MODEL_WIDTH, KV_COLS), ((0, 8), (1, 4)), -0.2, 0.2)), 0.1, 1.0),
        "gradient": noise(splits[9], (MODEL_WIDTH, KV_COLS), 1.0, 6.0, ((0, 8), (1, 4)), jnp.float32),
    }


beta_first = 0.9
beta_second = 0.999
correct_first = 0.9999734386011124
correct_second = 0.09520785288629038
adam_eps = 1e-08
learn_rate = 0.003
decay_rate = 0.1
norm_eps = 1e-06
rope_base = 1000000.0

def rotate(keys, positions):
    halfway = keys.shape[-1] // 2
    frequency = rope_base ** (-(jnp.arange(halfway, dtype=jnp.float32) * 2.0 / keys.shape[-1]))
    angles = positions[:, :, None] * frequency[None, None, :]
    cosine = jnp.cos(angles)[:, :, None, :]
    sine = jnp.sin(angles)[:, :, None, :]
    first_half = keys[..., :halfway]
    second_half = keys[..., halfway:]
    return jnp.concatenate([first_half * cosine - second_half * sine, second_half * cosine + first_half * sine], axis=-1)

def attention(queries, rotated_key_cache, head_value_cache, key_new, value_new, lengths):
    batch_rows, steps = (queries.shape[0], queries.shape[1])
    window = rotated_key_cache.shape[1]
    kv_heads = rotated_key_cache.shape[2] // HEAD_SIZE
    sharing_factor = QUERY_HEADS // KEY_VALUE_HEADS
    factor = HEAD_SIZE ** (-0.5)
    query_heads = queries.reshape(batch_rows, steps, kv_heads, sharing_factor, HEAD_SIZE).astype(jnp.float32)
    cache_key_seeds = rotated_key_cache.reshape(batch_rows, window, kv_heads, HEAD_SIZE).astype(jnp.float32)
    cache_values = head_value_cache.reshape(batch_rows, window, kv_heads, HEAD_SIZE).astype(jnp.float32)
    scores_cached = jnp.einsum('rsxgd,rlxd->rxgsl', query_heads, cache_key_seeds) * factor
    scores_fresh = jnp.einsum('rsxgd,ruxd->rxgsu', query_heads, key_new.astype(jnp.float32)) * factor
    present = (jnp.arange(window, dtype=jnp.int32)[None, :] < lengths[:, None])[:, None, None, None, :]
    causal = (jnp.arange(steps, dtype=jnp.int32)[None, :] <= jnp.arange(steps, dtype=jnp.int32)[:, None])[None, None, None, :, :]
    scores_cached = jnp.where(present, scores_cached, -jnp.inf)
    scores_fresh = jnp.where(causal, scores_fresh, -jnp.inf)
    ceiling = jnp.maximum(lax.optimization_barrier(jnp.max(scores_cached, axis=-1, keepdims=True)), lax.optimization_barrier(jnp.max(scores_fresh, axis=-1, keepdims=True)))
    probs_cached = jnp.exp(scores_cached - ceiling)
    probs_fresh = jnp.exp(scores_fresh - ceiling)
    denom = lax.optimization_barrier(jnp.sum(probs_cached, axis=-1, keepdims=True)) + lax.optimization_barrier(jnp.sum(probs_fresh, axis=-1, keepdims=True))
    weights_cached = probs_cached.astype(jnp.bfloat16).astype(jnp.float32)
    weights_fresh = probs_fresh.astype(jnp.bfloat16).astype(jnp.float32)
    blended = jnp.einsum('rxgsl,rlxd->rsxgd', weights_cached, cache_values)
    blended = blended + jnp.einsum('rxgsu,ruxd->rsxgd', weights_fresh, value_new.astype(jnp.float32))
    blended = blended / jnp.transpose(denom, (0, 3, 1, 2, 4))
    return blended.astype(jnp.bfloat16).reshape(batch_rows, steps, kv_heads * sharing_factor * HEAD_SIZE)

def reference(tokens, norm_gain, queries, rotated_key_cache, head_value_cache, lengths, master, moment_first, moment_second, gradient):
    average = beta_first * moment_first + (1.0 - beta_first) * gradient
    variance = beta_second * moment_second + (1.0 - beta_second) * gradient * gradient
    update = average / correct_first / (jnp.sqrt(variance / correct_second) + adam_eps)
    renewed = master - learn_rate * (update + decay_rate * master)
    layer_half = renewed.astype(jnp.bfloat16)
    gain_wide = norm_gain.astype(jnp.float32)

    def replica(bundle):
        replica_tokens, replica_queries, replica_keys, replica_values, replica_lengths = bundle
        widened = replica_tokens.astype(jnp.float32)
        mean_square = lax.optimization_barrier(jnp.sum(widened * widened, axis=-1, keepdims=True)) / MODEL_WIDTH
        normed = (widened * lax.rsqrt(mean_square + norm_eps) * gain_wide).astype(jnp.bfloat16)
        projected_output = jnp.dot(normed.reshape(REPLICA_ROWS * NEW_TOKENS, MODEL_WIDTH), layer_half, preferred_element_type=jnp.float32)
        projected_output = projected_output.reshape(REPLICA_ROWS, NEW_TOKENS, KEY_VALUE_HEADS, 2, HEAD_SIZE)
        positions = (replica_lengths[:, None] + jnp.arange(NEW_TOKENS, dtype=jnp.int32)[None, :]).astype(jnp.float32)
        key_new = rotate(projected_output[:, :, :, 0, :], positions).astype(jnp.bfloat16)
        value_new = projected_output[:, :, :, 1, :].astype(jnp.bfloat16)
        appended = jnp.stack([key_new, value_new], axis=3).reshape(REPLICA_ROWS, NEW_TOKENS, KV_COLS)
        attended = attention(replica_queries, replica_keys, replica_values, key_new, value_new, replica_lengths)
        return (attended, appended)
    grouped_bundles = (tokens.reshape(N_GRP, REPLICA_ROWS, NEW_TOKENS, MODEL_WIDTH), queries.reshape(N_GRP, REPLICA_ROWS, NEW_TOKENS, QUERY_HEADS * HEAD_SIZE), rotated_key_cache.reshape(N_GRP, REPLICA_ROWS, CACHE_SLOTS, KEY_VALUE_HEADS * HEAD_SIZE), head_value_cache.reshape(N_GRP, REPLICA_ROWS, CACHE_SLOTS, KEY_VALUE_HEADS * HEAD_SIZE), lengths.reshape(N_GRP, REPLICA_ROWS))
    attended, appended = lax.map(replica, grouped_bundles)
    attended = attended.reshape(TOTAL_ROWS, NEW_TOKENS, QUERY_HEADS * HEAD_SIZE)
    appended = appended.reshape(TOTAL_ROWS, NEW_TOKENS, KV_COLS)
    return (attended, appended, renewed, average, variance)
```

```python
import functools

import jax
import jax.numpy as jnp
from jax import lax
from jax.experimental import pallas as pl
from jax.experimental.pallas import tpu as pltpu
from jax.sharding import PartitionSpec as P

MESH_ID = pl.DeviceIdType.MESH
PIECES = 4
ADAM_PARTS = 8
AHEAD = 2
LEAD = 3
LAG = 2
LAG_GATE = 2

MODEL_WIDTH = 8192
QUERY_HEADS = 64
KEY_VALUE_HEADS = 8
HEAD_SIZE = 128


beta_first = 0.9
beta_second = 0.999
correct_first = 0.9999734386011124
correct_second = 0.09520785288629038
adam_eps = 1e-08
learn_rate = 0.003
decay_rate = 0.1
norm_eps = 1e-06
rope_base = 1000000.0


def rotate(keys, positions):
    halfway = keys.shape[-1] // 2
    frequency = rope_base ** (-(jnp.arange(halfway, dtype=jnp.float32) * 2.0 / keys.shape[-1]))
    angles = positions[:, :, None] * frequency[None, None, :]
    cosine = jnp.cos(angles)[:, :, None, :]
    sine = jnp.sin(angles)[:, :, None, :]
    first_half = keys[..., :halfway]
    second_half = keys[..., halfway:]
    return jnp.concatenate(
        [first_half * cosine - second_half * sine, second_half * cosine + first_half * sine],
        axis=-1,
    )


def attention(queries, rotated_key_cache, head_value_cache, key_new, value_new, lengths):
    batch_rows, steps = (queries.shape[0], queries.shape[1])
    window = rotated_key_cache.shape[1]
    kv_heads = rotated_key_cache.shape[2] // HEAD_SIZE
    sharing_factor = QUERY_HEADS // KEY_VALUE_HEADS
    factor = HEAD_SIZE ** (-0.5)
    query_heads = queries.reshape(batch_rows, steps, kv_heads, sharing_factor, HEAD_SIZE)
    cache_key_seeds = rotated_key_cache.reshape(batch_rows, window, kv_heads, HEAD_SIZE)
    cache_values = head_value_cache.reshape(batch_rows, window, kv_heads, HEAD_SIZE)
    scores_cached = (
        jnp.einsum(
            "rsxgd,rlxd->rxgsl", query_heads, cache_key_seeds, preferred_element_type=jnp.float32
        )
        * factor
    )
    scores_fresh = (
        jnp.einsum("rsxgd,ruxd->rxgsu", query_heads, key_new, preferred_element_type=jnp.float32)
        * factor
    )
    present = (jnp.arange(window, dtype=jnp.int32)[None, :] < lengths[:, None])[
        :, None, None, None, :
    ]
    causal = (
        jnp.arange(steps, dtype=jnp.int32)[None, :] <= jnp.arange(steps, dtype=jnp.int32)[:, None]
    )[None, None, None, :, :]
    scores_cached = jnp.where(present, scores_cached, -jnp.inf)
    scores_fresh = jnp.where(causal, scores_fresh, -jnp.inf)
    ceiling = jnp.maximum(
        jnp.max(scores_cached, axis=-1, keepdims=True),
        jnp.max(scores_fresh, axis=-1, keepdims=True),
    )
    probs_cached = jnp.exp(scores_cached - ceiling)
    probs_fresh = jnp.exp(scores_fresh - ceiling)
    denom = jnp.sum(probs_cached, axis=-1, keepdims=True) + jnp.sum(
        probs_fresh, axis=-1, keepdims=True
    )
    weights_cached = probs_cached.astype(jnp.bfloat16)
    weights_fresh = probs_fresh.astype(jnp.bfloat16)
    blended = jnp.einsum(
        "rxgsl,rlxd->rsxgd", weights_cached, cache_values, preferred_element_type=jnp.float32
    )
    blended = blended + jnp.einsum(
        "rxgsu,ruxd->rsxgd", weights_fresh, value_new, preferred_element_type=jnp.float32
    )
    blended = blended / jnp.transpose(denom, (0, 3, 1, 2, 4))
    return blended.astype(jnp.bfloat16).reshape(
        batch_rows, steps, kv_heads * sharing_factor * HEAD_SIZE
    )


def exchange_kernel(sizes, tok_ref, gain_ref, cos_ref, sin_ref, present_ref, q_hbm, k_hbm, v_hbm, mas_hbm, fir_hbm, sec_hbm,
                    gra_hbm, out_ref, app_ref, mas_ref, fir_ref, sec_ref, gra_ref, w_ref, sent, transit, held, squares,
                    squares_in, scale_ref, total, pair_out, pair_in, near_out, near_in, mid_out, mid_in, far_out, far_in,
                    q_ref, k_ref, v_ref, part_out, part_max, part_sum, sq_s, sq_r, tok_s, tok_r, tr_r, rl_s, fx_s, fc_s,
                    pair_s, pair_r, near_s, near_r, mid_s, mid_r, far_s, far_r, load_s, adam_s):
    grp, tp, fs = sizes
    line = grp // 2
    g, t, f = lax.axis_index("grp"), lax.axis_index("tp"), lax.axis_index("fs")
    z, y = g // 2, lax.rem(g, 2)
    rows, width = tok_ref.shape
    depth = w_ref.shape[0]
    blocks = width // depth
    piece = rows // PIECES
    me = t * fs + f
    owner_t, owner_f = z // fs, lax.rem(z, fs)
    half_z, side = z // 2, lax.rem(z, 2)
    near = half_z * 2 + 1 - side
    gate = side != half_z
    far_gate = 2 - half_z
    far_outer = 3 * (1 - half_z)
    zs_of = (z, near, far_gate, far_outer)

    def remote(src, dst, ss, rs, device):
        return pltpu.make_async_remote_copy(
            src_ref=src, dst_ref=dst, send_sem=ss, recv_sem=rs, device_id=device, device_id_type=MESH_ID
        )

    barrier = pltpu.get_barrier_semaphore()
    mates = [(g, 1 - t, f), (g, t, 1 - f), (g, 1 - t, 1 - f)]
    peers = [(lax.rem(g + i, grp), t, k) for i in range(1, grp) for k in (f, 1 - f)]
    loads = [
        pltpu.make_async_copy(src, dst, load_s.at[i])
        for i, (src, dst) in enumerate(((q_hbm, q_ref), (k_hbm, k_ref), (v_hbm, v_ref)))
    ]
    part_rows = depth // ADAM_PARTS
    adam_loads = [
        [
            pltpu.make_async_copy(src.at[pl.ds(a * part_rows, part_rows)], dst.at[pl.ds(a * part_rows, part_rows)], adam_s.at[a, i])
            for i, (src, dst) in enumerate(((mas_hbm, mas_ref), (fir_hbm, fir_ref), (sec_hbm, sec_ref), (gra_hbm, gra_ref)))
        ]
        for a in range(ADAM_PARTS)
    ]
    for device in peers + mates:
        pl.semaphore_signal(barrier, inc=1, device_id=device, device_id_type=MESH_ID)
    for copies in adam_loads:
        for copy in copies:
            copy.start()
    for copy in loads:
        copy.start()

    def fill(c):
        window = pl.ds(c * piece, piece)
        for j in range(blocks):
            cols = pl.ds(j * depth, depth)
            sent[c, j] = (tok_ref[window, cols].astype(jnp.float32) * gain_ref[:, cols].astype(jnp.float32)).astype(
                jnp.bfloat16
            )

    def send(c, end):
        for turn in range(2):
            j = lax.rem(y + c + turn, 2)
            dest = me * blocks + j
            src = sent.at[c, j]
            away = remote(src, held.at[c, g], tok_s.at[c, turn], tok_r.at[c, g], (dest, t, f))
            cross = remote(src, transit.at[c], tok_s.at[c, turn], tr_r.at[c], mates[1])
            direct = (dest != g) if turn == 0 else (dest != g) & (me == z)

            @pl.when(direct)
            def _():
                away.wait_send() if end else away.start()

            if turn == 1:

                @pl.when(me != z)
                def _():
                    cross.wait_send() if end else cross.start()

            if not end:

                @pl.when(dest == g)
                def _():
                    pltpu.make_async_copy(src, held.at[c, g], tok_r.at[c, g]).start()

    other = t * fs + 1 - f

    def relay(c, end):
        j = lax.rem(y + c + 1, 2)
        copy = remote(transit.at[c], held.at[c, g], rl_s.at[c], tok_r.at[c, g], (other * blocks + j, t, f))

        @pl.when(other != z)
        def _():
            if end:
                copy.wait_send()
            else:
                remote(transit.at[c], transit.at[c], rl_s.at[c], tr_r.at[c], mates[1]).wait_recv()
                copy.start()

    def forward(c, i, end):
        for turn in range(2):
            slot = zs_of[i] * 2 + lax.rem(y + c + turn, 2)
            first_f = owner_f if i == 0 or turn == 0 else 1 - owner_f
            block = held.at[c, slot]
            across = remote(block, block, fx_s.at[c, 2 * i + turn], tok_r.at[c, slot], mates[1])
            beside = remote(block, block, fc_s.at[c, 2 * i + turn], tok_r.at[c, slot], mates[0])
            if not end:
                across.wait_recv()

            @pl.when((t == owner_t) & (f == first_f))
            def _():
                across.wait_send() if end else across.start()

            @pl.when(t == owner_t)
            def _():
                beside.wait_send() if end else beside.start()

    def adam(a):
        for copy in adam_loads[a]:
            copy.wait()
        few_rows = 32

        def body(r, carry):
            window = pl.ds(pl.multiple_of(a * part_rows + r * few_rows, few_rows), few_rows)
            slope, old = gra_ref[window, :], mas_ref[window, :]
            average = beta_first * fir_ref[window, :] + (1.0 - beta_first) * slope
            variance = beta_second * sec_ref[window, :] + (1.0 - beta_second) * slope * slope
            update = average / correct_first / (jnp.sqrt(variance / correct_second) + adam_eps)
            renewed = old - learn_rate * (update + decay_rate * old)
            fir_ref[window, :] = average
            sec_ref[window, :] = variance
            mas_ref[window, :] = renewed
            w_ref[window, :] = renewed.astype(jnp.bfloat16)
            return carry

        lax.fori_loop(0, part_rows // few_rows, body, 0)

    sq = [remote(squares, squares_in.at[i], sq_s.at[i], sq_r.at[i], mates[i]) for i in range(3)]

    def start_squares():
        for c in range(PIECES):
            wide = tok_ref[pl.ds(c * piece, piece), :].astype(jnp.float32)
            wide = wide * wide
            part = wide[:, :128]
            for i in range(1, width // 128):
                part = part + wide[:, i * 128 : (i + 1) * 128]
            scale_ref[pl.ds(c * piece, piece), :] = part
        squares[...] = jnp.broadcast_to(jnp.sum(scale_ref[...].T, axis=0, keepdims=True), squares.shape)
        for copy in sq:
            copy.start()

    def finish_squares():
        for copy in sq:
            copy.wait()
        summed = (squares[...] + squares_in[0]) + (squares_in[1] + squares_in[2])
        scale = lax.rsqrt(summed / (width * tp * fs) + norm_eps)
        scale_ref[...] = jnp.broadcast_to(scale[0:1], (128, rows)).T

    def pair_copy(c, i):
        return remote(pair_out.at[c, i], pair_in.at[c, i], pair_s.at[c, i], pair_r.at[c, i], (z * 2 + 1 - y, t, f))

    def near_copy(c):
        return remote(near_out.at[c], near_in.at[c], near_s.at[c], near_r.at[c], (near * 2 + y, t, f))

    def mid_copy(c, k):
        return remote(mid_out.at[c, k], mid_in.at[c, k], mid_s.at[c, k], mid_r.at[c, k], (near * 2 + y, t, f))

    def far_copy(c, k):
        return remote(far_out.at[c, k], far_in.at[c], far_s.at[c, k], far_r.at[c], (zs_of[2 + k] * 2 + y, t, f))

    def multiply(c, i):
        slots2 = held[c, pl.ds(zs_of[i] * 2, 2)].reshape(2 * piece, depth)
        product = jnp.dot(slots2, w_ref[...], preferred_element_type=jnp.float32)
        total[c, i] = product.reshape(2, piece, product.shape[1])
        pair_out[c, i] = total[c, i, 1 - y].astype(jnp.bfloat16)
        pair_copy(c, i).start()

    def combine(c, i):
        pair_copy(c, i).wait_recv()
        both = total[c, i, y] + pair_in[c, i].astype(jnp.float32)
        if i == 0:
            total[c, 0, 0] = both
        elif i == 1:
            near_out[c] = both.astype(jnp.bfloat16)
            near_copy(c).start()
        else:

            @pl.when(gate)
            def _():
                total[c, i, 0] = both

            @pl.when(jnp.logical_not(gate))
            def _():
                mid_out[c, i - 2] = both.astype(jnp.bfloat16)
                mid_copy(c, i - 2).start()

    def pass_on(c, i):
        if i >= 2:

            @pl.when(gate)
            def _():
                mid_copy(c, i - 2).wait_recv()
                far_out[c, i - 2] = (total[c, i, 0] + mid_in[c, i - 2].astype(jnp.float32)).astype(jnp.bfloat16)
                far_copy(c, i - 2).start()

    batch_rows, slots, kv_width = k_ref.shape
    steps = rows // batch_rows
    kv_heads = kv_width // HEAD_SIZE
    share = q_ref.shape[1] // kv_width
    few = 128 // slots
    band = few * steps
    factor = HEAD_SIZE ** (-0.5)
    chunks = batch_rows // few
    over_last = (((1,), (1,)), ((), ()))

    def head_lanes(x, h):
        return pl.ds((x * share + h) * HEAD_SIZE, HEAD_SIZE)

    def some_queries(b, x):
        return jnp.concatenate([q_ref[pl.ds(b * band, band), head_lanes(x, h)] for h in range(share)], axis=0)

    def attend_cached(b):
        shape = (share * band, few * slots)
        row = lax.rem(lax.broadcasted_iota(jnp.int32, shape, 0), band) // steps
        same = row == lax.broadcasted_iota(jnp.int32, shape, 1) // slots
        valid = same & (present_ref[pl.ds(b, 1), :] > 0.5)
        for x in range(kv_heads):
            lanes = pl.ds(x * HEAD_SIZE, HEAD_SIZE)
            keys = k_ref[pl.ds(b * few, few), :, lanes].reshape(few * slots, HEAD_SIZE)
            values = v_ref[pl.ds(b * few, few), :, lanes].reshape(few * slots, HEAD_SIZE)
            scores = (
                lax.dot_general(some_queries(b, x), keys, over_last, preferred_element_type=jnp.float32) * factor
            )
            scores = jnp.where(valid, scores, -jnp.inf)
            most = jnp.max(scores, axis=1, keepdims=True)
            probs = jnp.exp(scores - most)
            part_max[b, x] = jnp.broadcast_to(most, (share * band, HEAD_SIZE))
            part_sum[b, x] = jnp.broadcast_to(jnp.sum(probs, axis=1, keepdims=True), (share * band, HEAD_SIZE))
            part_out[b, x] = jnp.dot(probs.astype(jnp.bfloat16), values, preferred_element_type=jnp.float32)

    def attend_new(b):
        shape = (share * band, band)
        mine = lax.rem(lax.broadcasted_iota(jnp.int32, shape, 0), band)
        other_row = lax.broadcasted_iota(jnp.int32, shape, 1)
        valid = (mine // steps == other_row // steps) & (other_row <= mine)
        window = pl.ds(b * band, band)
        for x in range(kv_heads):
            keys = app_ref[window, pl.ds(2 * x * HEAD_SIZE, HEAD_SIZE)]
            values = app_ref[window, pl.ds((2 * x + 1) * HEAD_SIZE, HEAD_SIZE)]
            scores = (
                lax.dot_general(some_queries(b, x), keys, over_last, preferred_element_type=jnp.float32) * factor
            )
            scores = jnp.where(valid, scores, -jnp.inf)
            before = part_max[b, x]
            most = jnp.maximum(before, jnp.max(scores, axis=1, keepdims=True))
            probs = jnp.exp(scores - most[:, :1])
            again = jnp.exp(before - most)
            denom = again * part_sum[b, x] + jnp.sum(probs, axis=1, keepdims=True)
            blended = again * part_out[b, x] + jnp.dot(
                probs.astype(jnp.bfloat16), values, preferred_element_type=jnp.float32
            )
            blended = (blended / denom).astype(jnp.bfloat16)
            for h in range(share):
                out_ref[window, head_lanes(x, h)] = blended[h * band : (h + 1) * band]

    half = HEAD_SIZE // 2

    def finish(c):
        window = pl.ds(c * piece, piece)
        near_copy(c).wait_recv()
        far_copy(c, 0).wait_recv()
        scale = scale_ref[window, :]
        for x in range(kv_heads):
            lanes = pl.ds(2 * x * HEAD_SIZE, HEAD_SIZE)
            later = pl.ds((2 * x + 1) * HEAD_SIZE, HEAD_SIZE)

            def summed(cols):
                arrived = near_in[c, :, cols].astype(jnp.float32) + far_in[c, :, cols].astype(jnp.float32)
                return (total[c, 0, 0, :, cols] + arrived) * scale

            key = summed(lanes)
            key = key * cos_ref[window, :] + pltpu.roll(key, half, 1) * sin_ref[window, :]
            app_ref[window, lanes] = key.astype(jnp.bfloat16)
            app_ref[window, later] = summed(later).astype(jnp.bfloat16)
        for b in range(c * chunks // PIECES, (c + 1) * chunks // PIECES):
            attend_new(b)

    for c in range(AHEAD):
        fill(c)
    pl.semaphore_wait(barrier, len(peers) + len(mates))
    for c in range(AHEAD):
        send(c, False)
    for c in range(AHEAD, PIECES):
        fill(c)
    start_squares()

    order = [(c, i) for c in range(PIECES) for i in ((0, 1, 2, 3) if c == 0 else (2, 3, 1, 0))]
    count = len(order)

    def arrive(n):
        c, i = order[n]
        if n % line == 0:
            if c == 0:
                relay(0, False)
            if c + AHEAD < PIECES:
                send(c + AHEAD, False)
            if c + 1 < PIECES:
                relay(c + 1, False)
        forward(c, i, False)

    for a in range(ADAM_PARTS):
        adam(a)
        k = a - (ADAM_PARTS - LEAD)
        if k >= 0:
            arrive(k)
    finish_squares()
    for copy in loads:
        copy.wait()
    done = 0
    finished = 0
    steps_now = -(-chunks // (count - 4))
    for n in range(count + LAG + LAG_GATE):
        if n + LEAD < count:
            arrive(n + LEAD)
        if n < count:
            multiply(*order[n])
        if LAG <= n < count + LAG:
            combine(*order[n - LAG])
        for b in range(done, min(done + steps_now, chunks)):
            attend_cached(b)
        done = min(done + steps_now, chunks)
        if LAG + LAG_GATE <= n:
            pass_on(*order[n - LAG - LAG_GATE])
            if (n - LAG - LAG_GATE) % line == line - 1 and (n - LAG - LAG_GATE) // line >= 1:
                finish((n - LAG - LAG_GATE) // line - 1)
    finish(PIECES - 1)

    for c in range(PIECES):
        send(c, True)
        relay(c, True)
        for i in range(line):
            forward(c, i, True)
            pair_copy(c, i).wait_send()
        near_copy(c).wait_send()
        for k in range(2):

            @pl.when(gate)
            def _():
                far_copy(c, k).wait_send()

            @pl.when(jnp.logical_not(gate))
            def _():
                mid_copy(c, k).wait_send()


def project_and_attend(sizes, tokens, norm_gain, queries, key_cache, value_cache, lengths, master, moment_first, moment_second,
                       gradient):
    grp, _, _ = sizes
    batch_rows, steps, width = tokens.shape
    _, slots, kv_width = key_cache.shape
    rows = batch_rows * steps
    depth, columns = master.shape
    blocks, line = width // depth, grp // 2
    kv_heads, share = kv_width // HEAD_SIZE, queries.shape[2] // kv_width
    few = 128 // slots
    half = HEAD_SIZE // 2
    piece = rows // PIECES
    positions = (lengths[:, None] + jnp.arange(steps, dtype=jnp.int32)[None, :]).astype(jnp.float32)
    frequency = rope_base ** (-(jnp.arange(half, dtype=jnp.float32) * 2.0 / HEAD_SIZE))
    angles = positions.reshape(rows, 1) * frequency[None, :]
    cosine, sine = jnp.cos(angles), jnp.sin(angles)
    cosine = jnp.concatenate([cosine, cosine], axis=1)
    sine = jnp.concatenate([-sine, sine], axis=1)
    present = (jnp.arange(slots, dtype=jnp.int32)[None, :] < lengths[:, None]).astype(jnp.float32)
    present = present.reshape(batch_rows // few, few * slots)
    dma = pltpu.SemaphoreType.DMA
    vmem = pl.BlockSpec(memory_space=pltpu.VMEM)
    anywhere = pl.BlockSpec(memory_space=pl.ANY)
    flat_queries = queries.reshape(rows, queries.shape[2])
    part = pltpu.VMEM((batch_rows // few, kv_heads, share * few * steps, HEAD_SIZE), jnp.float32)
    state = jax.ShapeDtypeStruct(master.shape, jnp.float32)

    def half_width(*lead):
        return pltpu.VMEM((PIECES, *lead, piece, columns), jnp.bfloat16)

    attended, appended, renewed, average, variance = pl.pallas_call(
        functools.partial(exchange_kernel, sizes),
        out_shape=(
            jax.ShapeDtypeStruct(flat_queries.shape, jnp.bfloat16),
            jax.ShapeDtypeStruct((rows, columns), jnp.bfloat16),
            state,
            state,
            state,
        ),
        in_specs=[vmem] * 5 + [anywhere] * 7,
        out_specs=(vmem,) * 5,
        scratch_shapes=[
            pltpu.VMEM(master.shape, jnp.float32),
            pltpu.VMEM(master.shape, jnp.bfloat16),
            pltpu.VMEM((PIECES, blocks, piece, depth), jnp.bfloat16),
            pltpu.VMEM((PIECES, piece, depth), jnp.bfloat16),
            pltpu.VMEM((PIECES, grp, piece, depth), jnp.bfloat16),
            pltpu.VMEM((8, rows), jnp.float32),
            pltpu.VMEM((3, 8, rows), jnp.float32),
            pltpu.VMEM((rows, 128), jnp.float32),
            pltpu.VMEM((PIECES, line, 2, piece, columns), jnp.float32),
            half_width(line),
            half_width(line),
            half_width(),
            half_width(),
            half_width(2),
            half_width(2),
            half_width(2),
            half_width(),
            pltpu.VMEM(flat_queries.shape, jnp.bfloat16),
            pltpu.VMEM(key_cache.shape, jnp.bfloat16),
            pltpu.VMEM(value_cache.shape, jnp.bfloat16),
            part,
            part,
            part,
            dma((3,)),
            dma((3,)),
            dma((PIECES, 2)),
            dma((PIECES, grp)),
            dma((PIECES,)),
            dma((PIECES,)),
            dma((PIECES, grp)),
            dma((PIECES, grp)),
            dma((PIECES, line)),
            dma((PIECES, line)),
            dma((PIECES,)),
            dma((PIECES,)),
            dma((PIECES, 2)),
            dma((PIECES, 2)),
            dma((PIECES, 2)),
            dma((PIECES,)),
            dma((3,)),
            dma((ADAM_PARTS, 4)),
        ],
        compiler_params=pltpu.CompilerParams(collective_id=0, has_side_effects=True, vmem_limit_bytes=40 << 20),
    )(
        tokens.reshape(rows, width), norm_gain.reshape(1, width), cosine, sine, present, flat_queries, key_cache, value_cache,
        master, moment_first, moment_second, gradient,
    )
    return attended.reshape(queries.shape), appended.reshape(batch_rows, steps, columns), renewed, average, variance


def fits(sizes, tokens, master, queries, key_cache):
    grp, tp, fs = sizes
    batch_rows, steps, width = tokens.shape
    rows, depth, columns = batch_rows * steps, master.shape[0], master.shape[1]
    slots, kv_width = key_cache.shape[1:]
    if tp != 2 or fs != 2 or grp != 2 * tp * fs or width != 2 * depth or 128 % slots or slots % 16:
        return False
    few = 128 // slots
    return (
        depth % (32 * ADAM_PARTS) == 0 and depth % 128 == 0 and rows % 128 == 0 and rows % (16 * PIECES) == 0
        and columns == 2 * kv_width and few * steps % 16 == 0 and batch_rows % (few * PIECES) == 0
        and queries.shape[2] % kv_width == 0
    )


def project_gathered(tokens, norm_gain, layer_half):
    batch_rows, steps = (tokens.shape[0], tokens.shape[1])
    widened, gain_whole = (
        lax.all_gather(tokens, ("tp", "fs"), axis=2, tiled=True),
        lax.all_gather(norm_gain, ("tp", "fs"), axis=0, tiled=True),
    )
    mean_square = (
        jnp.einsum("rsd,rsd->rs", widened, widened, preferred_element_type=jnp.float32)[..., None]
        / MODEL_WIDTH
    )
    normed = (widened * lax.rsqrt(mean_square + norm_eps) * gain_whole.astype(jnp.float32)).astype(
        jnp.bfloat16
    )
    flattened = normed.reshape(batch_rows * steps, MODEL_WIDTH)
    gathered = lax.all_gather(layer_half, "grp", axis=0, tiled=True)
    return jnp.dot(flattened, gathered, preferred_element_type=jnp.float32)


def shards(
    sizes,
    tokens,
    norm_gain,
    queries,
    rotated_key_cache,
    head_value_cache,
    lengths,
    master,
    moment_first,
    moment_second,
    gradient,
):
    if fits(sizes, tokens, master, queries, rotated_key_cache):
        return project_and_attend(
            sizes, tokens, norm_gain, queries, rotated_key_cache, head_value_cache, lengths, master, moment_first, moment_second,
            gradient,
        )
    average = beta_first * moment_first + (1.0 - beta_first) * gradient
    variance = beta_second * moment_second + (1.0 - beta_second) * gradient * gradient
    update = average / correct_first / (jnp.sqrt(variance / correct_second) + adam_eps)
    renewed = master - learn_rate * (update + decay_rate * master)
    layer_half = renewed.astype(jnp.bfloat16)
    batch_rows, steps = (tokens.shape[0], tokens.shape[1])
    columns = layer_half.shape[1]
    projected_output = project_gathered(tokens, norm_gain, layer_half)
    kv_heads = columns // (2 * HEAD_SIZE)
    projected_output = projected_output.reshape(batch_rows, steps, kv_heads, 2, HEAD_SIZE)
    positions = (lengths[:, None] + jnp.arange(steps, dtype=jnp.int32)[None, :]).astype(jnp.float32)
    key_new = rotate(projected_output[:, :, :, 0, :], positions).astype(jnp.bfloat16)
    value_new = projected_output[:, :, :, 1, :].astype(jnp.bfloat16)
    appended = jnp.stack([key_new, value_new], axis=3).reshape(batch_rows, steps, columns)
    attended = attention(queries, rotated_key_cache, head_value_cache, key_new, value_new, lengths)
    return (attended, appended, renewed, average, variance)


def solution(mesh):
    in_specs = (
        P("grp", None, ("tp", "fs")),
        P(("tp", "fs")),
        P("grp", None, ("tp", "fs")),
        P("grp", None, ("tp", "fs")),
        P("grp", None, ("tp", "fs")),
        P("grp"),
        P("grp", ("tp", "fs")),
        P("grp", ("tp", "fs")),
        P("grp", ("tp", "fs")),
        P("grp", ("tp", "fs")),
    )
    out_specs = (
        P("grp", None, ("tp", "fs")),
        P("grp", None, ("tp", "fs")),
        P("grp", ("tp", "fs")),
        P("grp", ("tp", "fs")),
        P("grp", ("tp", "fs")),
    )
    return jax.shard_map(
        functools.partial(shards, tuple(mesh.shape[name] for name in ("grp", "tp", "fs"))), mesh=mesh, in_specs=in_specs, out_specs=out_specs, check_vma=False,
    )
```

```python
import functools

import jax
import jax.numpy as jnp
from jax import lax
from jax.experimental import pallas as pl
from jax.experimental.pallas import tpu as pltpu
from jax.sharding import PartitionSpec as P

MESH_ID = pl.DeviceIdType.MESH
PIECES = 4
ADAM_PARTS = 8
AHEAD = 2
LEAD = 5
NEXT = 1
LAG = 2
LAG_GATE = 2

MODEL_WIDTH = 8192
QUERY_HEADS = 64
KEY_VALUE_HEADS = 8
HEAD_SIZE = 128


beta_first = 0.9
beta_second = 0.999
correct_first = 0.9999734386011124
correct_second = 0.09520785288629038
adam_eps = 1e-08
learn_rate = 0.003
decay_rate = 0.1
norm_eps = 1e-06
rope_base = 1000000.0


def rotate(keys, positions):
    halfway = keys.shape[-1] // 2
    frequency = rope_base ** (-(jnp.arange(halfway, dtype=jnp.float32) * 2.0 / keys.shape[-1]))
    angles = positions[:, :, None] * frequency[None, None, :]
    cosine = jnp.cos(angles)[:, :, None, :]
    sine = jnp.sin(angles)[:, :, None, :]
    first_half = keys[..., :halfway]
    second_half = keys[..., halfway:]
    return jnp.concatenate(
        [first_half * cosine - second_half * sine, second_half * cosine + first_half * sine],
        axis=-1,
    )


def attention(queries, rotated_key_cache, head_value_cache, key_new, value_new, lengths):
    batch_rows, steps = (queries.shape[0], queries.shape[1])
    window = rotated_key_cache.shape[1]
    kv_heads = rotated_key_cache.shape[2] // HEAD_SIZE
    sharing_factor = QUERY_HEADS // KEY_VALUE_HEADS
    factor = HEAD_SIZE ** (-0.5)
    query_heads = queries.reshape(batch_rows, steps, kv_heads, sharing_factor, HEAD_SIZE)
    cache_key_seeds = rotated_key_cache.reshape(batch_rows, window, kv_heads, HEAD_SIZE)
    cache_values = head_value_cache.reshape(batch_rows, window, kv_heads, HEAD_SIZE)
    scores_cached = (
        jnp.einsum(
            "rsxgd,rlxd->rxgsl", query_heads, cache_key_seeds, preferred_element_type=jnp.float32
        )
        * factor
    )
    scores_fresh = (
        jnp.einsum("rsxgd,ruxd->rxgsu", query_heads, key_new, preferred_element_type=jnp.float32)
        * factor
    )
    present = (jnp.arange(window, dtype=jnp.int32)[None, :] < lengths[:, None])[
        :, None, None, None, :
    ]
    causal = (
        jnp.arange(steps, dtype=jnp.int32)[None, :] <= jnp.arange(steps, dtype=jnp.int32)[:, None]
    )[None, None, None, :, :]
    scores_cached = jnp.where(present, scores_cached, -jnp.inf)
    scores_fresh = jnp.where(causal, scores_fresh, -jnp.inf)
    ceiling = jnp.maximum(
        jnp.max(scores_cached, axis=-1, keepdims=True),
        jnp.max(scores_fresh, axis=-1, keepdims=True),
    )
    probs_cached = jnp.exp(scores_cached - ceiling)
    probs_fresh = jnp.exp(scores_fresh - ceiling)
    denom = jnp.sum(probs_cached, axis=-1, keepdims=True) + jnp.sum(
        probs_fresh, axis=-1, keepdims=True
    )
    weights_cached = probs_cached.astype(jnp.bfloat16)
    weights_fresh = probs_fresh.astype(jnp.bfloat16)
    blended = jnp.einsum(
        "rxgsl,rlxd->rsxgd", weights_cached, cache_values, preferred_element_type=jnp.float32
    )
    blended = blended + jnp.einsum(
        "rxgsu,ruxd->rsxgd", weights_fresh, value_new, preferred_element_type=jnp.float32
    )
    blended = blended / jnp.transpose(denom, (0, 3, 1, 2, 4))
    return blended.astype(jnp.bfloat16).reshape(
        batch_rows, steps, kv_heads * sharing_factor * HEAD_SIZE
    )


def exchange_kernel(sizes, tok_ref, gain_ref, cos_ref, sin_ref, present_ref, q_hbm, k_hbm, v_hbm, mas_hbm, fir_hbm, sec_hbm,
                    gra_hbm, out_ref, app_ref, mas_ref, fir_ref, sec_ref, gra_ref, w_ref, sent, transit, held, squares,
                    squares_in, scale_ref, total, pair_out, pair_in, near_out, near_in, mid_out, mid_in, far_out, far_in,
                    q_ref, k_ref, v_ref, part_out, part_max, part_sum, sq_s, sq_r, tok_s, tok_r, tr_r, rl_s, fx_s, fc_s,
                    pair_s, pair_r, near_s, near_r, mid_s, mid_r, far_s, far_r, load_s, adam_s):
    grp, tp, fs = sizes
    line = grp // 2
    g, t, f = lax.axis_index("grp"), lax.axis_index("tp"), lax.axis_index("fs")
    z, y = g // 2, lax.rem(g, 2)
    rows, width = tok_ref.shape
    depth = w_ref.shape[0]
    blocks = width // depth
    piece = rows // PIECES
    me = t * fs + f
    owner_t, owner_f = z // fs, lax.rem(z, fs)
    half_z, side = z // 2, lax.rem(z, 2)
    near = half_z * 2 + 1 - side
    gate = side != half_z
    far_gate = 2 - half_z
    far_outer = 3 * (1 - half_z)
    zs_of = (z, near, far_gate, far_outer)

    def remote(src, dst, ss, rs, device):
        return pltpu.make_async_remote_copy(
            src_ref=src, dst_ref=dst, send_sem=ss, recv_sem=rs, device_id=device, device_id_type=MESH_ID
        )

    barrier = pltpu.get_barrier_semaphore()
    mates = [(g, 1 - t, f), (g, t, 1 - f), (g, 1 - t, 1 - f)]
    peers = [(lax.rem(g + i, grp), t, k) for i in range(1, grp) for k in (f, 1 - f)]
    loads = [
        pltpu.make_async_copy(src, dst, load_s.at[i])
        for i, (src, dst) in enumerate(((q_hbm, q_ref), (k_hbm, k_ref), (v_hbm, v_ref)))
    ]
    part_rows = depth // ADAM_PARTS
    adam_loads = [
        [
            pltpu.make_async_copy(src.at[pl.ds(a * part_rows, part_rows)], dst.at[pl.ds(a * part_rows, part_rows)], adam_s.at[a, i])
            for i, (src, dst) in enumerate(((mas_hbm, mas_ref), (fir_hbm, fir_ref), (sec_hbm, sec_ref), (gra_hbm, gra_ref)))
        ]
        for a in range(ADAM_PARTS)
    ]
    for device in peers + mates:
        pl.semaphore_signal(barrier, inc=1, device_id=device, device_id_type=MESH_ID)
    for copies in adam_loads:
        for copy in copies:
            copy.start()
    for copy in loads:
        copy.start()

    def fill(c):
        window = pl.ds(c * piece, piece)
        for j in range(blocks):
            cols = pl.ds(j * depth, depth)
            sent[c, j] = (tok_ref[window, cols].astype(jnp.float32) * gain_ref[:, cols].astype(jnp.float32)).astype(
                jnp.bfloat16
            )

    def send(c, end):
        for turn in range(2):
            j = lax.rem(y + c + turn, 2)
            dest = me * blocks + j
            src = sent.at[c, j]
            away = remote(src, held.at[c, g], tok_s.at[c, turn], tok_r.at[c, g], (dest, t, f))
            cross = remote(src, transit.at[c], tok_s.at[c, turn], tr_r.at[c], mates[1])
            direct = (dest != g) if turn == 0 else (dest != g) & (me == z)

            @pl.when(direct)
            def _():
                away.wait_send() if end else away.start()

            if turn == 1:

                @pl.when(me != z)
                def _():
                    cross.wait_send() if end else cross.start()

            if not end:

                @pl.when(dest == g)
                def _():
                    pltpu.make_async_copy(src, held.at[c, g], tok_r.at[c, g]).start()

    other = t * fs + 1 - f

    def relay(c, end):
        j = lax.rem(y + c + 1, 2)
        copy = remote(transit.at[c], held.at[c, g], rl_s.at[c], tok_r.at[c, g], (other * blocks + j, t, f))

        @pl.when(other != z)
        def _():
            if end:
                copy.wait_send()
            else:
                remote(transit.at[c], transit.at[c], rl_s.at[c], tr_r.at[c], mates[1]).wait_recv()
                copy.start()

    def slot_copies(c, i, turn):
        slot = zs_of[i] * 2 + lax.rem(y + c + turn, 2)
        first_f = owner_f if i == 0 or turn == 0 else 1 - owner_f
        block = held.at[c, slot]
        across = remote(block, block, fx_s.at[c, 2 * i + turn], tok_r.at[c, slot], mates[1])
        beside = remote(block, block, fc_s.at[c, 2 * i + turn], tok_r.at[c, slot], mates[0])
        return across, beside, first_f

    def lead(c, i):
        for turn in range(2):
            across, beside, first_f = slot_copies(c, i, turn)

            @pl.when((t == owner_t) & (f == first_f))
            def _():
                across.wait_recv()
                across.start()
                beside.start()

    def second(c, i):
        for turn in range(2):
            across, beside, first_f = slot_copies(c, i, turn)

            @pl.when((t == owner_t) & (f != first_f))
            def _():
                across.wait_recv()
                beside.start()

    def third(c, i):
        for turn in range(2):
            across, _, _ = slot_copies(c, i, turn)

            @pl.when(t != owner_t)
            def _():
                across.wait_recv()

    def sent_on(c, i):
        for turn in range(2):
            across, beside, first_f = slot_copies(c, i, turn)

            @pl.when((t == owner_t) & (f == first_f))
            def _():
                across.wait_send()

            @pl.when(t == owner_t)
            def _():
                beside.wait_send()

    def adam(a):
        for copy in adam_loads[a]:
            copy.wait()
        few_rows = 32

        def body(r, carry):
            window = pl.ds(pl.multiple_of(a * part_rows + r * few_rows, few_rows), few_rows)
            slope, old = gra_ref[window, :], mas_ref[window, :]
            average = beta_first * fir_ref[window, :] + (1.0 - beta_first) * slope
            variance = beta_second * sec_ref[window, :] + (1.0 - beta_second) * slope * slope
            update = average / correct_first / (jnp.sqrt(variance / correct_second) + adam_eps)
            renewed = old - learn_rate * (update + decay_rate * old)
            fir_ref[window, :] = average
            sec_ref[window, :] = variance
            mas_ref[window, :] = renewed
            w_ref[window, :] = renewed.astype(jnp.bfloat16)
            return carry

        lax.fori_loop(0, part_rows // few_rows, body, 0)

    sq = [remote(squares, squares_in.at[i], sq_s.at[i], sq_r.at[i], mates[i]) for i in range(3)]

    def start_squares():
        for c in range(PIECES):
            wide = tok_ref[pl.ds(c * piece, piece), :].astype(jnp.float32)
            wide = wide * wide
            part = wide[:, :128]
            for i in range(1, width // 128):
                part = part + wide[:, i * 128 : (i + 1) * 128]
            scale_ref[pl.ds(c * piece, piece), :] = part
        squares[...] = jnp.broadcast_to(jnp.sum(scale_ref[...].T, axis=0, keepdims=True), squares.shape)
        for copy in sq:
            copy.start()

    def finish_squares():
        for copy in sq:
            copy.wait()
        summed = (squares[...] + squares_in[0]) + (squares_in[1] + squares_in[2])
        scale = lax.rsqrt(summed / (width * tp * fs) + norm_eps)
        scale_ref[...] = jnp.broadcast_to(scale[0:1], (128, rows)).T

    def pair_copy(c, i):
        return remote(pair_out.at[c, i], pair_in.at[c, i], pair_s.at[c, i], pair_r.at[c, i], (z * 2 + 1 - y, t, f))

    def near_copy(c):
        return remote(near_out.at[c], near_in.at[c], near_s.at[c], near_r.at[c], (near * 2 + y, t, f))

    def mid_copy(c, k):
        return remote(mid_out.at[c, k], mid_in.at[c, k], mid_s.at[c, k], mid_r.at[c, k], (near * 2 + y, t, f))

    def far_copy(c, k):
        return remote(far_out.at[c, k], far_in.at[c], far_s.at[c, k], far_r.at[c], (zs_of[2 + k] * 2 + y, t, f))

    def multiply(c, i):
        slots2 = held[c, pl.ds(zs_of[i] * 2, 2)].reshape(2 * piece, depth)
        product = jnp.dot(slots2, w_ref[...], preferred_element_type=jnp.float32)
        total[c, i] = product.reshape(2, piece, product.shape[1])
        pair_out[c, i] = total[c, i, 1 - y].astype(jnp.bfloat16)
        pair_copy(c, i).start()

    def combine(c, i):
        pair_copy(c, i).wait_recv()
        both = total[c, i, y] + pair_in[c, i].astype(jnp.float32)
        if i == 0:
            total[c, 0, 0] = both
        elif i == 1:
            near_out[c] = both.astype(jnp.bfloat16)
            near_copy(c).start()
        else:

            @pl.when(gate)
            def _():
                total[c, i, 0] = both

            @pl.when(jnp.logical_not(gate))
            def _():
                mid_out[c, i - 2] = both.astype(jnp.bfloat16)
                mid_copy(c, i - 2).start()

    def pass_on(c, i):
        if i >= 2:

            @pl.when(gate)
            def _():
                mid_copy(c, i - 2).wait_recv()
                far_out[c, i - 2] = (total[c, i, 0] + mid_in[c, i - 2].astype(jnp.float32)).astype(jnp.bfloat16)
                far_copy(c, i - 2).start()

    batch_rows, slots, kv_width = k_ref.shape
    steps = rows // batch_rows
    kv_heads = kv_width // HEAD_SIZE
    share = q_ref.shape[1] // kv_width
    few = 128 // slots
    band = few * steps
    factor = HEAD_SIZE ** (-0.5)
    chunks = batch_rows // few
    over_last = (((1,), (1,)), ((), ()))

    def head_lanes(x, h):
        return pl.ds((x * share + h) * HEAD_SIZE, HEAD_SIZE)

    def some_queries(b, x):
        return jnp.concatenate([q_ref[pl.ds(b * band, band), head_lanes(x, h)] for h in range(share)], axis=0)

    def attend_cached(b):
        shape = (share * band, few * slots)
        row = lax.rem(lax.broadcasted_iota(jnp.int32, shape, 0), band) // steps
        same = row == lax.broadcasted_iota(jnp.int32, shape, 1) // slots
        valid = same & (present_ref[pl.ds(b, 1), :] > 0.5)
        for x in range(kv_heads):
            lanes = pl.ds(x * HEAD_SIZE, HEAD_SIZE)
            keys = k_ref[pl.ds(b * few, few), :, lanes].reshape(few * slots, HEAD_SIZE)
            values = v_ref[pl.ds(b * few, few), :, lanes].reshape(few * slots, HEAD_SIZE)
            scores = (
                lax.dot_general(some_queries(b, x), keys, over_last, preferred_element_type=jnp.float32) * factor
            )
            scores = jnp.where(valid, scores, -jnp.inf)
            most = jnp.max(scores, axis=1, keepdims=True)
            probs = jnp.exp(scores - most)
            part_max[b, x] = jnp.broadcast_to(most, (share * band, HEAD_SIZE))
            part_sum[b, x] = jnp.broadcast_to(jnp.sum(probs, axis=1, keepdims=True), (share * band, HEAD_SIZE))
            part_out[b, x] = jnp.dot(probs.astype(jnp.bfloat16), values, preferred_element_type=jnp.float32)

    def attend_new(b):
        shape = (share * band, band)
        mine = lax.rem(lax.broadcasted_iota(jnp.int32, shape, 0), band)
        other_row = lax.broadcasted_iota(jnp.int32, shape, 1)
        valid = (mine // steps == other_row // steps) & (other_row <= mine)
        window = pl.ds(b * band, band)
        for x in range(kv_heads):
            keys = app_ref[window, pl.ds(2 * x * HEAD_SIZE, HEAD_SIZE)]
            values = app_ref[window, pl.ds((2 * x + 1) * HEAD_SIZE, HEAD_SIZE)]
            scores = (
                lax.dot_general(some_queries(b, x), keys, over_last, preferred_element_type=jnp.float32) * factor
            )
            scores = jnp.where(valid, scores, -jnp.inf)
            before = part_max[b, x]
            most = jnp.maximum(before, jnp.max(scores, axis=1, keepdims=True))
            probs = jnp.exp(scores - most[:, :1])
            again = jnp.exp(before - most)
            denom = again * part_sum[b, x] + jnp.sum(probs, axis=1, keepdims=True)
            blended = again * part_out[b, x] + jnp.dot(
                probs.astype(jnp.bfloat16), values, preferred_element_type=jnp.float32
            )
            blended = (blended / denom).astype(jnp.bfloat16)
            for h in range(share):
                out_ref[window, head_lanes(x, h)] = blended[h * band : (h + 1) * band]

    half = HEAD_SIZE // 2

    def finish(c):
        window = pl.ds(c * piece, piece)
        near_copy(c).wait_recv()
        far_copy(c, 0).wait_recv()
        scale = scale_ref[window, :]
        for x in range(kv_heads):
            lanes = pl.ds(2 * x * HEAD_SIZE, HEAD_SIZE)
            later = pl.ds((2 * x + 1) * HEAD_SIZE, HEAD_SIZE)

            def summed(cols):
                arrived = near_in[c, :, cols].astype(jnp.float32) + far_in[c, :, cols].astype(jnp.float32)
                return (total[c, 0, 0, :, cols] + arrived) * scale

            key = summed(lanes)
            key = key * cos_ref[window, :] + pltpu.roll(key, half, 1) * sin_ref[window, :]
            app_ref[window, lanes] = key.astype(jnp.bfloat16)
            app_ref[window, later] = summed(later).astype(jnp.bfloat16)
        for b in range(c * chunks // PIECES, (c + 1) * chunks // PIECES):
            attend_new(b)

    for c in range(AHEAD):
        fill(c)
    pl.semaphore_wait(barrier, len(peers) + len(mates))
    for c in range(AHEAD):
        send(c, False)
    for c in range(AHEAD, PIECES):
        fill(c)
    start_squares()

    order = [(c, i) for c in range(PIECES) for i in ((0, 1, 2, 3) if c == 0 else (2, 3, 1, 0))]
    count = len(order)

    def arrive(n):
        c, i = order[n]
        if n % line == 0:
            if c == 0:
                relay(0, False)
            if c + AHEAD < PIECES:
                send(c + AHEAD, False)
            if c + 1 < PIECES:
                relay(c + 1, False)
        lead(c, i)

    for n in range(LEAD):
        adam_until = (n + 1) * ADAM_PARTS // LEAD
        for a in range(n * ADAM_PARTS // LEAD, adam_until):
            adam(a)
        arrive(n)
        if n >= LEAD - NEXT:
            second(*order[n - LEAD + NEXT])
    finish_squares()
    for copy in loads:
        copy.wait()
    done = 0
    steps_now = -(-chunks // (count - 4))
    for n in range(count + LAG + LAG_GATE):
        if n + LEAD < count:
            arrive(n + LEAD)
        if n + NEXT < count:
            second(*order[n + NEXT])
        if n < count:
            third(*order[n])
            multiply(*order[n])
        if LAG <= n < count + LAG:
            combine(*order[n - LAG])
        for b in range(done, min(done + steps_now, chunks)):
            attend_cached(b)
        done = min(done + steps_now, chunks)
        if LAG + LAG_GATE <= n:
            m = n - LAG - LAG_GATE
            pass_on(*order[m])
            if m % line == line - 1 and m >= line:
                finish(m // line - 1)
    finish(PIECES - 1)

    for c in range(PIECES):
        send(c, True)
        relay(c, True)
        for i in range(line):
            sent_on(c, i)
            pair_copy(c, i).wait_send()
        near_copy(c).wait_send()
        for k in range(2):

            @pl.when(gate)
            def _():
                far_copy(c, k).wait_send()

            @pl.when(jnp.logical_not(gate))
            def _():
                mid_copy(c, k).wait_send()


def project_and_attend(sizes, tokens, norm_gain, queries, key_cache, value_cache, lengths, master, moment_first, moment_second,
                       gradient):
    grp, _, _ = sizes
    batch_rows, steps, width = tokens.shape
    _, slots, kv_width = key_cache.shape
    rows = batch_rows * steps
    depth, columns = master.shape
    blocks, line = width // depth, grp // 2
    kv_heads, share = kv_width // HEAD_SIZE, queries.shape[2] // kv_width
    few = 128 // slots
    half = HEAD_SIZE // 2
    piece = rows // PIECES
    positions = (lengths[:, None] + jnp.arange(steps, dtype=jnp.int32)[None, :]).astype(jnp.float32)
    frequency = rope_base ** (-(jnp.arange(half, dtype=jnp.float32) * 2.0 / HEAD_SIZE))
    angles = positions.reshape(rows, 1) * frequency[None, :]
    cosine, sine = jnp.cos(angles), jnp.sin(angles)
    cosine = jnp.concatenate([cosine, cosine], axis=1)
    sine = jnp.concatenate([-sine, sine], axis=1)
    present = (jnp.arange(slots, dtype=jnp.int32)[None, :] < lengths[:, None]).astype(jnp.float32)
    present = present.reshape(batch_rows // few, few * slots)
    dma = pltpu.SemaphoreType.DMA
    vmem = pl.BlockSpec(memory_space=pltpu.VMEM)
    anywhere = pl.BlockSpec(memory_space=pl.ANY)
    flat_queries = queries.reshape(rows, queries.shape[2])
    part = pltpu.VMEM((batch_rows // few, kv_heads, share * few * steps, HEAD_SIZE), jnp.float32)
    state = jax.ShapeDtypeStruct(master.shape, jnp.float32)

    def half_width(*lead):
        return pltpu.VMEM((PIECES, *lead, piece, columns), jnp.bfloat16)

    attended, appended, renewed, average, variance = pl.pallas_call(
        functools.partial(exchange_kernel, sizes),
        out_shape=(
            jax.ShapeDtypeStruct(flat_queries.shape, jnp.bfloat16),
            jax.ShapeDtypeStruct((rows, columns), jnp.bfloat16),
            state,
            state,
            state,
        ),
        in_specs=[vmem] * 5 + [anywhere] * 7,
        out_specs=(vmem,) * 5,
        scratch_shapes=[
            pltpu.VMEM(master.shape, jnp.float32),
            pltpu.VMEM(master.shape, jnp.bfloat16),
            pltpu.VMEM((PIECES, blocks, piece, depth), jnp.bfloat16),
            pltpu.VMEM((PIECES, piece, depth), jnp.bfloat16),
            pltpu.VMEM((PIECES, grp, piece, depth), jnp.bfloat16),
            pltpu.VMEM((8, rows), jnp.float32),
            pltpu.VMEM((3, 8, rows), jnp.float32),
            pltpu.VMEM((rows, 128), jnp.float32),
            pltpu.VMEM((PIECES, line, 2, piece, columns), jnp.float32),
            half_width(line),
            half_width(line),
            half_width(),
            half_width(),
            half_width(2),
            half_width(2),
            half_width(2),
            half_width(),
            pltpu.VMEM(flat_queries.shape, jnp.bfloat16),
            pltpu.VMEM(key_cache.shape, jnp.bfloat16),
            pltpu.VMEM(value_cache.shape, jnp.bfloat16),
            part,
            part,
            part,
            dma((3,)),
            dma((3,)),
            dma((PIECES, 2)),
            dma((PIECES, grp)),
            dma((PIECES,)),
            dma((PIECES,)),
            dma((PIECES, grp)),
            dma((PIECES, grp)),
            dma((PIECES, line)),
            dma((PIECES, line)),
            dma((PIECES,)),
            dma((PIECES,)),
            dma((PIECES, 2)),
            dma((PIECES, 2)),
            dma((PIECES, 2)),
            dma((PIECES,)),
            dma((3,)),
            dma((ADAM_PARTS, 4)),
        ],
        compiler_params=pltpu.CompilerParams(collective_id=0, has_side_effects=True, vmem_limit_bytes=40 << 20),
    )(
        tokens.reshape(rows, width), norm_gain.reshape(1, width), cosine, sine, present, flat_queries, key_cache, value_cache,
        master, moment_first, moment_second, gradient,
    )
    return attended.reshape(queries.shape), appended.reshape(batch_rows, steps, columns), renewed, average, variance


def fits(sizes, tokens, master, queries, key_cache):
    grp, tp, fs = sizes
    batch_rows, steps, width = tokens.shape
    rows, depth, columns = batch_rows * steps, master.shape[0], master.shape[1]
    slots, kv_width = key_cache.shape[1:]
    if tp != 2 or fs != 2 or grp != 2 * tp * fs or width != 2 * depth or 128 % slots or slots % 16:
        return False
    few = 128 // slots
    return (
        depth % (32 * ADAM_PARTS) == 0 and depth % 128 == 0 and rows % 128 == 0 and rows % (16 * PIECES) == 0
        and columns == 2 * kv_width and few * steps % 16 == 0 and batch_rows % (few * PIECES) == 0
        and queries.shape[2] % kv_width == 0
    )


def project_gathered(tokens, norm_gain, layer_half):
    batch_rows, steps = (tokens.shape[0], tokens.shape[1])
    widened, gain_whole = (
        lax.all_gather(tokens, ("tp", "fs"), axis=2, tiled=True),
        lax.all_gather(norm_gain, ("tp", "fs"), axis=0, tiled=True),
    )
    mean_square = (
        jnp.einsum("rsd,rsd->rs", widened, widened, preferred_element_type=jnp.float32)[..., None]
        / MODEL_WIDTH
    )
    normed = (widened * lax.rsqrt(mean_square + norm_eps) * gain_whole.astype(jnp.float32)).astype(
        jnp.bfloat16
    )
    flattened = normed.reshape(batch_rows * steps, MODEL_WIDTH)
    gathered = lax.all_gather(layer_half, "grp", axis=0, tiled=True)
    return jnp.dot(flattened, gathered, preferred_element_type=jnp.float32)


def shards(
    sizes,
    tokens,
    norm_gain,
    queries,
    rotated_key_cache,
    head_value_cache,
    lengths,
    master,
    moment_first,
    moment_second,
    gradient,
):
    if fits(sizes, tokens, master, queries, rotated_key_cache):
        return project_and_attend(
            sizes, tokens, norm_gain, queries, rotated_key_cache, head_value_cache, lengths, master, moment_first, moment_second,
            gradient,
        )
    average = beta_first * moment_first + (1.0 - beta_first) * gradient
    variance = beta_second * moment_second + (1.0 - beta_second) * gradient * gradient
    update = average / correct_first / (jnp.sqrt(variance / correct_second) + adam_eps)
    renewed = master - learn_rate * (update + decay_rate * master)
    layer_half = renewed.astype(jnp.bfloat16)
    batch_rows, steps = (tokens.shape[0], tokens.shape[1])
    columns = layer_half.shape[1]
    projected_output = project_gathered(tokens, norm_gain, layer_half)
    kv_heads = columns // (2 * HEAD_SIZE)
    projected_output = projected_output.reshape(batch_rows, steps, kv_heads, 2, HEAD_SIZE)
    positions = (lengths[:, None] + jnp.arange(steps, dtype=jnp.int32)[None, :]).astype(jnp.float32)
    key_new = rotate(projected_output[:, :, :, 0, :], positions).astype(jnp.bfloat16)
    value_new = projected_output[:, :, :, 1, :].astype(jnp.bfloat16)
    appended = jnp.stack([key_new, value_new], axis=3).reshape(batch_rows, steps, columns)
    attended = attention(queries, rotated_key_cache, head_value_cache, key_new, value_new, lengths)
    return (attended, appended, renewed, average, variance)


def solution(mesh):
    in_specs = (
        P("grp", None, ("tp", "fs")),
        P(("tp", "fs")),
        P("grp", None, ("tp", "fs")),
        P("grp", None, ("tp", "fs")),
        P("grp", None, ("tp", "fs")),
        P("grp"),
        P("grp", ("tp", "fs")),
        P("grp", ("tp", "fs")),
        P("grp", ("tp", "fs")),
        P("grp", ("tp", "fs")),
    )
    out_specs = (
        P("grp", None, ("tp", "fs")),
        P("grp", None, ("tp", "fs")),
        P("grp", ("tp", "fs")),
        P("grp", ("tp", "fs")),
        P("grp", ("tp", "fs")),
    )
    return jax.shard_map(
        functools.partial(shards, tuple(mesh.shape[name] for name in ("grp", "tp", "fs"))), mesh=mesh, in_specs=in_specs, out_specs=out_specs, check_vma=False,
    )
```

```python
import functools
import math

import jax
import jax.numpy as jnp
from jax import lax
from jax.experimental import pallas as pl
from jax.experimental.pallas import tpu as pltpu
from jax.sharding import PartitionSpec as P

MESH_ID = pl.DeviceIdType.MESH
PIECES = 4
ADAM_PARTS = 8
AHEAD = 2
LEAD = 5
NEXT = 1
LAG = 2
LAG_GATE = 2

MODEL_WIDTH = 8192
QUERY_HEADS = 64
KEY_VALUE_HEADS = 8
HEAD_SIZE = 128


beta_first = 0.9
beta_second = 0.999
correct_first = 0.9999734386011124
correct_second = 0.09520785288629038
adam_eps = 1e-08
learn_rate = 0.003
decay_rate = 0.1
norm_eps = 1e-06
rope_base = 1000000.0


def rotate(keys, positions):
    halfway = keys.shape[-1] // 2
    frequency = rope_base ** (-(jnp.arange(halfway, dtype=jnp.float32) * 2.0 / keys.shape[-1]))
    angles = positions[:, :, None] * frequency[None, None, :]
    cosine = jnp.cos(angles)[:, :, None, :]
    sine = jnp.sin(angles)[:, :, None, :]
    first_half = keys[..., :halfway]
    second_half = keys[..., halfway:]
    return jnp.concatenate(
        [first_half * cosine - second_half * sine, second_half * cosine + first_half * sine],
        axis=-1,
    )


def attention(queries, rotated_key_cache, head_value_cache, key_new, value_new, lengths):
    batch_rows, steps = (queries.shape[0], queries.shape[1])
    window = rotated_key_cache.shape[1]
    kv_heads = rotated_key_cache.shape[2] // HEAD_SIZE
    sharing_factor = QUERY_HEADS // KEY_VALUE_HEADS
    factor = HEAD_SIZE ** (-0.5)
    query_heads = queries.reshape(batch_rows, steps, kv_heads, sharing_factor, HEAD_SIZE)
    cache_key_seeds = rotated_key_cache.reshape(batch_rows, window, kv_heads, HEAD_SIZE)
    cache_values = head_value_cache.reshape(batch_rows, window, kv_heads, HEAD_SIZE)
    scores_cached = (
        jnp.einsum(
            "rsxgd,rlxd->rxgsl", query_heads, cache_key_seeds, preferred_element_type=jnp.float32
        )
        * factor
    )
    scores_fresh = (
        jnp.einsum("rsxgd,ruxd->rxgsu", query_heads, key_new, preferred_element_type=jnp.float32)
        * factor
    )
    present = (jnp.arange(window, dtype=jnp.int32)[None, :] < lengths[:, None])[
        :, None, None, None, :
    ]
    causal = (
        jnp.arange(steps, dtype=jnp.int32)[None, :] <= jnp.arange(steps, dtype=jnp.int32)[:, None]
    )[None, None, None, :, :]
    scores_cached = jnp.where(present, scores_cached, -jnp.inf)
    scores_fresh = jnp.where(causal, scores_fresh, -jnp.inf)
    ceiling = jnp.maximum(
        jnp.max(scores_cached, axis=-1, keepdims=True),
        jnp.max(scores_fresh, axis=-1, keepdims=True),
    )
    probs_cached = jnp.exp(scores_cached - ceiling)
    probs_fresh = jnp.exp(scores_fresh - ceiling)
    denom = jnp.sum(probs_cached, axis=-1, keepdims=True) + jnp.sum(
        probs_fresh, axis=-1, keepdims=True
    )
    weights_cached = probs_cached.astype(jnp.bfloat16)
    weights_fresh = probs_fresh.astype(jnp.bfloat16)
    blended = jnp.einsum(
        "rxgsl,rlxd->rsxgd", weights_cached, cache_values, preferred_element_type=jnp.float32
    )
    blended = blended + jnp.einsum(
        "rxgsu,ruxd->rsxgd", weights_fresh, value_new, preferred_element_type=jnp.float32
    )
    blended = blended / jnp.transpose(denom, (0, 3, 1, 2, 4))
    return blended.astype(jnp.bfloat16).reshape(
        batch_rows, steps, kv_heads * sharing_factor * HEAD_SIZE
    )


def exchange_kernel(sizes, tok_hbm, gain_hbm, len_ref, q_hbm, k_hbm, v_hbm, mas_hbm, fir_hbm, sec_hbm, gra_hbm, out_ref,
                    new_ref, mas_ref, fir_ref, sec_ref, tok_ref, gain_ref, cos_ref, sin_ref, present_ref, app_ref, gra_ref, w_ref,
                    sent, transit, held, squares, squares_in, scale_ref, total, pair_out, pair_in, near_out, near_in, mid_out,
                    mid_in, far_out, far_in, q_ref, k_ref, v_ref, part_out, part_max, part_sum, sq_s, sq_r, tok_s, tok_r, tr_r,
                    rl_s, fx_s, fc_s, pair_s, pair_r, near_s, near_r, mid_s, mid_r, far_s, far_r, load_s, adam_s, first_s):
    grp, tp, fs = sizes
    line = grp // 2
    g, t, f = lax.axis_index("grp"), lax.axis_index("tp"), lax.axis_index("fs")
    z, y = g // 2, lax.rem(g, 2)
    batch_rows, steps, width = tok_ref.shape
    rows = batch_rows * steps
    depth = w_ref.shape[0]
    blocks = width // depth
    piece = rows // PIECES
    lot = batch_rows // PIECES
    me = t * fs + f
    owner_t, owner_f = z // fs, lax.rem(z, fs)
    half_z, side = z // 2, lax.rem(z, 2)
    near = half_z * 2 + 1 - side
    gate = side != half_z
    far_gate = 2 - half_z
    far_outer = 3 * (1 - half_z)
    zs_of = (z, near, far_gate, far_outer)

    def remote(src, dst, ss, rs, device):
        return pltpu.make_async_remote_copy(
            src_ref=src, dst_ref=dst, send_sem=ss, recv_sem=rs, device_id=device, device_id_type=MESH_ID
        )

    barrier = pltpu.get_barrier_semaphore()
    mates = [(g, 1 - t, f), (g, t, 1 - f), (g, 1 - t, 1 - f)]
    peers = [(lax.rem(g + i, grp), t, k) for i in range(1, grp) for k in (f, 1 - f)]
    loads = [
        pltpu.make_async_copy(src, dst, load_s.at[i])
        for i, (src, dst) in enumerate(((q_hbm, q_ref), (k_hbm, k_ref), (v_hbm, v_ref)))
    ]
    part_rows = depth // ADAM_PARTS
    adam_loads = [
        [
            pltpu.make_async_copy(src.at[pl.ds(a * part_rows, part_rows)], dst.at[pl.ds(a * part_rows, part_rows)], adam_s.at[a, i])
            for i, (src, dst) in enumerate(((mas_hbm, mas_ref), (fir_hbm, fir_ref), (sec_hbm, sec_ref), (gra_hbm, gra_ref)))
        ]
        for a in range(ADAM_PARTS)
    ]
    first = [pltpu.make_async_copy(gain_hbm, gain_ref, first_s.at[PIECES])] + [
        pltpu.make_async_copy(tok_hbm.at[pl.ds(c * lot, lot)], tok_ref.at[pl.ds(c * lot, lot)], first_s.at[c])
        for c in range(PIECES)
    ]
    for copy in first:
        copy.start()
    for device in peers + mates:
        pl.semaphore_signal(barrier, inc=1, device_id=device, device_id_type=MESH_ID)
    for copies in adam_loads:
        for copy in copies:
            copy.start()
    for copy in loads:
        copy.start()

    def tokens_of(c, cols):
        return tok_ref[pl.ds(c * lot, lot), :, cols].reshape(piece, cols.size).astype(jnp.float32)

    def fill(c):
        for copy in first[: 2] if c == 0 else first[c + 1 : c + 2]:
            copy.wait()
        for j in range(blocks):
            cols = pl.ds(j * depth, depth)
            gain = gain_ref[:, cols].astype(jnp.float32)
            sent[c, j] = (tokens_of(c, cols) * gain).astype(jnp.bfloat16)

    def send(c, end):
        for turn in range(2):
            j = lax.rem(y + c + turn, 2)
            dest = me * blocks + j
            src = sent.at[c, j]
            away = remote(src, held.at[c, g], tok_s.at[c, turn], tok_r.at[c, g], (dest, t, f))
            cross = remote(src, transit.at[c], tok_s.at[c, turn], tr_r.at[c], mates[1])
            direct = (dest != g) if turn == 0 else (dest != g) & (me == z)

            @pl.when(direct)
            def _():
                away.wait_send() if end else away.start()

            if turn == 1:

                @pl.when(me != z)
                def _():
                    cross.wait_send() if end else cross.start()

            if not end:

                @pl.when(dest == g)
                def _():
                    pltpu.make_async_copy(src, held.at[c, g], tok_r.at[c, g]).start()

    other = t * fs + 1 - f

    def relay(c, end):
        j = lax.rem(y + c + 1, 2)
        copy = remote(transit.at[c], held.at[c, g], rl_s.at[c], tok_r.at[c, g], (other * blocks + j, t, f))

        @pl.when(other != z)
        def _():
            if end:
                copy.wait_send()
            else:
                remote(transit.at[c], transit.at[c], rl_s.at[c], tr_r.at[c], mates[1]).wait_recv()
                copy.start()

    def slot_copies(c, i, turn):
        slot = zs_of[i] * 2 + lax.rem(y + c + turn, 2)
        first_f = owner_f if i == 0 or turn == 0 else 1 - owner_f
        block = held.at[c, slot]
        across = remote(block, block, fx_s.at[c, 2 * i + turn], tok_r.at[c, slot], mates[1])
        beside = remote(block, block, fc_s.at[c, 2 * i + turn], tok_r.at[c, slot], mates[0])
        return across, beside, first_f

    def lead(c, i):
        for turn in range(2):
            across, beside, first_f = slot_copies(c, i, turn)

            @pl.when((t == owner_t) & (f == first_f))
            def _():
                across.wait_recv()
                across.start()
                beside.start()

    def second(c, i):
        for turn in range(2):
            across, beside, first_f = slot_copies(c, i, turn)

            @pl.when((t == owner_t) & (f != first_f))
            def _():
                across.wait_recv()
                beside.start()

    def third(c, i):
        for turn in range(2):
            across, _, _ = slot_copies(c, i, turn)

            @pl.when(t != owner_t)
            def _():
                across.wait_recv()

    def sent_on(c, i):
        for turn in range(2):
            across, beside, first_f = slot_copies(c, i, turn)

            @pl.when((t == owner_t) & (f == first_f))
            def _():
                across.wait_send()

            @pl.when(t == owner_t)
            def _():
                beside.wait_send()

    def adam(a):
        for copy in adam_loads[a]:
            copy.wait()
        few_rows = 32

        def body(r, carry):
            window = pl.ds(pl.multiple_of(a * part_rows + r * few_rows, few_rows), few_rows)
            slope, old = gra_ref[window, :], mas_ref[window, :]
            average = beta_first * fir_ref[window, :] + (1.0 - beta_first) * slope
            variance = beta_second * sec_ref[window, :] + (1.0 - beta_second) * slope * slope
            update = average / correct_first / (jnp.sqrt(variance / correct_second) + adam_eps)
            renewed = old - learn_rate * (update + decay_rate * old)
            fir_ref[window, :] = average
            sec_ref[window, :] = variance
            mas_ref[window, :] = renewed
            w_ref[window, :] = renewed.astype(jnp.bfloat16)
            return carry

        lax.fori_loop(0, part_rows // few_rows, body, 0)

    sq = [remote(squares, squares_in.at[i], sq_s.at[i], sq_r.at[i], mates[i]) for i in range(3)]

    def start_squares():
        for c in range(PIECES):
            wide = tokens_of(c, pl.ds(0, width))
            wide = wide * wide
            part = wide[:, :128]
            for i in range(1, width // 128):
                part = part + wide[:, i * 128 : (i + 1) * 128]
            scale_ref[pl.ds(c * piece, piece), :] = part
        squares[...] = jnp.broadcast_to(jnp.sum(scale_ref[...].T, axis=0, keepdims=True), squares.shape)
        for copy in sq:
            copy.start()

    def finish_squares():
        for copy in sq:
            copy.wait()
        summed = (squares[...] + squares_in[0]) + (squares_in[1] + squares_in[2])
        scale = lax.rsqrt(summed / (width * tp * fs) + norm_eps)
        scale_ref[...] = jnp.broadcast_to(scale[0:1], (128, rows)).T

    def pair_copy(c, i):
        return remote(pair_out.at[c, i], pair_in.at[c, i], pair_s.at[c, i], pair_r.at[c, i], (z * 2 + 1 - y, t, f))

    def near_copy(c):
        return remote(near_out.at[c], near_in.at[c], near_s.at[c], near_r.at[c], (near * 2 + y, t, f))

    def mid_copy(c, k):
        return remote(mid_out.at[c, k], mid_in.at[c, k], mid_s.at[c, k], mid_r.at[c, k], (near * 2 + y, t, f))

    def far_copy(c, k):
        return remote(far_out.at[c, k], far_in.at[c], far_s.at[c, k], far_r.at[c], (zs_of[2 + k] * 2 + y, t, f))

    def multiply(c, i):
        slots2 = held[c, pl.ds(zs_of[i] * 2, 2)].reshape(2 * piece, depth)
        product = jnp.dot(slots2, w_ref[...], preferred_element_type=jnp.float32)
        total[c, i] = product.reshape(2, piece, product.shape[1])
        pair_out[c, i] = total[c, i, 1 - y].astype(jnp.bfloat16)
        pair_copy(c, i).start()

    def combine(c, i):
        pair_copy(c, i).wait_recv()
        both = total[c, i, y] + pair_in[c, i].astype(jnp.float32)
        if i == 0:
            total[c, 0, 0] = both
        elif i == 1:
            near_out[c] = both.astype(jnp.bfloat16)
            near_copy(c).start()
        else:

            @pl.when(gate)
            def _():
                total[c, i, 0] = both

            @pl.when(jnp.logical_not(gate))
            def _():
                mid_out[c, i - 2] = both.astype(jnp.bfloat16)
                mid_copy(c, i - 2).start()

    def pass_on(c, i):
        if i >= 2:

            @pl.when(gate)
            def _():
                mid_copy(c, i - 2).wait_recv()
                far_out[c, i - 2] = (total[c, i, 0] + mid_in[c, i - 2].astype(jnp.float32)).astype(jnp.bfloat16)
                far_copy(c, i - 2).start()

    _, slots, kv_width = k_ref.shape
    kv_heads = kv_width // HEAD_SIZE
    share = q_ref.shape[2] // kv_width
    few = 128 // slots
    band = few * steps
    factor = HEAD_SIZE ** (-0.5)
    chunks = batch_rows // few
    over_last = (((1,), (1,)), ((), ()))

    def head_lanes(x, h):
        return pl.ds((x * share + h) * HEAD_SIZE, HEAD_SIZE)

    def some_queries(b, x):
        return jnp.concatenate(
            [q_ref[pl.ds(b * few, few), :, head_lanes(x, h)].reshape(band, HEAD_SIZE) for h in range(share)], axis=0
        )

    def attend_cached(b):
        shape = (share * band, few * slots)
        row = lax.rem(lax.broadcasted_iota(jnp.int32, shape, 0), band) // steps
        same = row == lax.broadcasted_iota(jnp.int32, shape, 1) // slots
        valid = same & (present_ref[pl.ds(b, 1), :] > 0.5)
        for x in range(kv_heads):
            lanes = pl.ds(x * HEAD_SIZE, HEAD_SIZE)
            keys = k_ref[pl.ds(b * few, few), :, lanes].reshape(few * slots, HEAD_SIZE)
            values = v_ref[pl.ds(b * few, few), :, lanes].reshape(few * slots, HEAD_SIZE)
            scores = (
                lax.dot_general(some_queries(b, x), keys, over_last, preferred_element_type=jnp.float32) * factor
            )
            scores = jnp.where(valid, scores, -jnp.inf)
            most = jnp.max(scores, axis=1, keepdims=True)
            probs = jnp.exp(scores - most)
            part_max[b, x] = jnp.broadcast_to(most, (share * band, HEAD_SIZE))
            part_sum[b, x] = jnp.broadcast_to(jnp.sum(probs, axis=1, keepdims=True), (share * band, HEAD_SIZE))
            part_out[b, x] = jnp.dot(probs.astype(jnp.bfloat16), values, preferred_element_type=jnp.float32)

    def attend_new(b):
        shape = (share * band, band)
        mine = lax.rem(lax.broadcasted_iota(jnp.int32, shape, 0), band)
        other_row = lax.broadcasted_iota(jnp.int32, shape, 1)
        valid = (mine // steps == other_row // steps) & (other_row <= mine)
        window = pl.ds(b * band, band)
        for x in range(kv_heads):
            keys = app_ref[window, pl.ds(2 * x * HEAD_SIZE, HEAD_SIZE)]
            values = app_ref[window, pl.ds((2 * x + 1) * HEAD_SIZE, HEAD_SIZE)]
            scores = (
                lax.dot_general(some_queries(b, x), keys, over_last, preferred_element_type=jnp.float32) * factor
            )
            scores = jnp.where(valid, scores, -jnp.inf)
            before = part_max[b, x]
            most = jnp.maximum(before, jnp.max(scores, axis=1, keepdims=True))
            probs = jnp.exp(scores - most[:, :1])
            again = jnp.exp(before - most)
            denom = again * part_sum[b, x] + jnp.sum(probs, axis=1, keepdims=True)
            blended = again * part_out[b, x] + jnp.dot(
                probs.astype(jnp.bfloat16), values, preferred_element_type=jnp.float32
            )
            blended = (blended / denom).astype(jnp.bfloat16)
            for h in range(share):
                out_ref[pl.ds(b * few, few), :, head_lanes(x, h)] = blended[h * band : (h + 1) * band].reshape(
                    few, steps, HEAD_SIZE
                )

    half = HEAD_SIZE // 2

    def prepare():
        lane = lax.broadcasted_iota(jnp.int32, (1, few * slots), 1)
        for b in range(chunks):
            lengths = jnp.full(lane.shape, len_ref[b * few], jnp.int32)
            for k in range(1, few):
                lengths = jnp.where(lane // slots == k, len_ref[b * few + k], lengths)
            present_ref[pl.ds(b, 1), :] = (lax.rem(lane, slots) < lengths).astype(jnp.float32)
        for b in range(batch_rows):
            cos_ref[pl.ds(b * steps, steps), :] = jnp.full((steps, HEAD_SIZE), len_ref[b].astype(jnp.float32))
        lane = lax.broadcasted_iota(jnp.int32, (8, HEAD_SIZE), 1)
        exponent = lax.rem(lane, half).astype(jnp.float32) * (2.0 / HEAD_SIZE)
        frequency = jnp.exp(exponent * (-math.log(rope_base)))
        sign = jnp.where(lane < half, -1.0, 1.0)
        step = lax.rem(lax.broadcasted_iota(jnp.int32, (8, HEAD_SIZE), 0), steps).astype(jnp.float32)

        def body(r, carry):
            window = pl.ds(pl.multiple_of(r * 8, 8), 8)
            angles = (cos_ref[window, :] + step) * frequency
            cos_ref[window, :] = jnp.cos(angles)
            sin_ref[window, :] = jnp.sin(angles) * sign
            return carry

        lax.fori_loop(0, rows // 8, body, 0)

    def finish(c):
        window = pl.ds(c * piece, piece)
        near_copy(c).wait_recv()
        far_copy(c, 0).wait_recv()
        scale = scale_ref[window, :]
        for x in range(kv_heads):
            lanes = pl.ds(2 * x * HEAD_SIZE, HEAD_SIZE)
            later = pl.ds((2 * x + 1) * HEAD_SIZE, HEAD_SIZE)

            def summed(cols):
                arrived = near_in[c, :, cols].astype(jnp.float32) + far_in[c, :, cols].astype(jnp.float32)
                return (total[c, 0, 0, :, cols] + arrived) * scale

            key = summed(lanes)
            key = key * cos_ref[window, :] + pltpu.roll(key, half, 1) * sin_ref[window, :]
            for cols, part in ((lanes, key), (later, summed(later))):
                part = part.astype(jnp.bfloat16)
                app_ref[window, cols] = part
                new_ref[pl.ds(c * lot, lot), :, cols] = part.reshape(lot, steps, HEAD_SIZE)
        for b in range(c * chunks // PIECES, (c + 1) * chunks // PIECES):
            attend_new(b)

    for c in range(AHEAD):
        fill(c)
    pl.semaphore_wait(barrier, len(peers) + len(mates))
    for c in range(AHEAD):
        send(c, False)
    for c in range(AHEAD, PIECES):
        fill(c)
    start_squares()
    prepare()

    order = [(c, i) for c in range(PIECES) for i in ((0, 1, 2, 3) if c == 0 else (2, 3, 1, 0))]
    count = len(order)

    def arrive(n):
        c, i = order[n]
        if n % line == 0:
            if c == 0:
                relay(0, False)
            if c + AHEAD < PIECES:
                send(c + AHEAD, False)
            if c + 1 < PIECES:
                relay(c + 1, False)
        lead(c, i)

    for n in range(LEAD):
        adam_until = (n + 1) * ADAM_PARTS // LEAD
        for a in range(n * ADAM_PARTS // LEAD, adam_until):
            adam(a)
        arrive(n)
        if n >= LEAD - NEXT:
            second(*order[n - LEAD + NEXT])
    finish_squares()
    for copy in loads:
        copy.wait()
    done = 0
    steps_now = -(-chunks // (count - 4))
    for n in range(count + LAG + LAG_GATE):
        if n + LEAD < count:
            arrive(n + LEAD)
        if n + NEXT < count:
            second(*order[n + NEXT])
        if n < count:
            third(*order[n])
            multiply(*order[n])
        if LAG <= n < count + LAG:
            combine(*order[n - LAG])
        for b in range(done, min(done + steps_now, chunks)):
            attend_cached(b)
        done = min(done + steps_now, chunks)
        if LAG + LAG_GATE <= n:
            m = n - LAG - LAG_GATE
            pass_on(*order[m])
            if m % line == line - 1 and m >= line:
                finish(m // line - 1)
    finish(PIECES - 1)

    for c in range(PIECES):
        send(c, True)
        relay(c, True)
        for i in range(line):
            sent_on(c, i)
            pair_copy(c, i).wait_send()
        near_copy(c).wait_send()
        for k in range(2):

            @pl.when(gate)
            def _():
                far_copy(c, k).wait_send()

            @pl.when(jnp.logical_not(gate))
            def _():
                mid_copy(c, k).wait_send()


def write_kernel(*refs):
    count = len(refs) // 2
    copies = [pltpu.make_async_copy(refs[i], refs[count + i], refs[-1].at[i]) for i in range(count)]
    for copy in copies:
        copy.start()
    for copy in copies:
        copy.wait()


def project_and_attend(sizes, tokens, norm_gain, queries, key_cache, value_cache, lengths, master, moment_first, moment_second,
                       gradient):
    grp, _, _ = sizes
    batch_rows, steps, width = tokens.shape
    _, slots, kv_width = key_cache.shape
    rows = batch_rows * steps
    depth, columns = master.shape
    blocks, line = width // depth, grp // 2
    kv_heads, share = kv_width // HEAD_SIZE, queries.shape[2] // kv_width
    few = 128 // slots
    piece = rows // PIECES
    dma = pltpu.SemaphoreType.DMA
    vmem = pl.BlockSpec(memory_space=pltpu.VMEM)
    anywhere = pl.BlockSpec(memory_space=pltpu.HBM)
    smem = pl.BlockSpec(memory_space=pltpu.SMEM)
    part = pltpu.VMEM((batch_rows // few, kv_heads, share * few * steps, HEAD_SIZE), jnp.float32)
    state = pltpu.VMEM(master.shape, jnp.float32)

    def placed(space, *arrays):
        return [pltpu.with_memory_space_constraint(array, space) for array in arrays]

    def half_width(*lead):
        return pltpu.VMEM((PIECES, *lead, piece, columns), jnp.bfloat16)

    results = pl.pallas_call(
        functools.partial(exchange_kernel, sizes),
        out_shape=(
            pltpu.VMEM(queries.shape, jnp.bfloat16),
            pltpu.VMEM((batch_rows, steps, columns), jnp.bfloat16),
            state,
            state,
            state,
        ),
        in_specs=[anywhere] * 2 + [smem] + [anywhere] * 7,
        out_specs=(vmem,) * 5,
        scratch_shapes=[
            pltpu.VMEM(tokens.shape, jnp.bfloat16),
            pltpu.VMEM((1, width), jnp.bfloat16),
            pltpu.VMEM((rows, HEAD_SIZE), jnp.float32),
            pltpu.VMEM((rows, HEAD_SIZE), jnp.float32),
            pltpu.VMEM((batch_rows // few, few * slots), jnp.float32),
            pltpu.VMEM((rows, columns), jnp.bfloat16),
            pltpu.VMEM(master.shape, jnp.float32),
            pltpu.VMEM(master.shape, jnp.bfloat16),
            pltpu.VMEM((PIECES, blocks, piece, depth), jnp.bfloat16),
            pltpu.VMEM((PIECES, piece, depth), jnp.bfloat16),
            pltpu.VMEM((PIECES, grp, piece, depth), jnp.bfloat16),
            pltpu.VMEM((8, rows), jnp.float32),
            pltpu.VMEM((3, 8, rows), jnp.float32),
            pltpu.VMEM((rows, 128), jnp.float32),
            pltpu.VMEM((PIECES, line, 2, piece, columns), jnp.float32),
            half_width(line),
            half_width(line),
            half_width(),
            half_width(),
            half_width(2),
            half_width(2),
            half_width(2),
            half_width(),
            pltpu.VMEM(queries.shape, jnp.bfloat16),
            pltpu.VMEM(key_cache.shape, jnp.bfloat16),
            pltpu.VMEM(value_cache.shape, jnp.bfloat16),
            part,
            part,
            part,
            dma((3,)),
            dma((3,)),
            dma((PIECES, 2)),
            dma((PIECES, grp)),
            dma((PIECES,)),
            dma((PIECES,)),
            dma((PIECES, grp)),
            dma((PIECES, grp)),
            dma((PIECES, line)),
            dma((PIECES, line)),
            dma((PIECES,)),
            dma((PIECES,)),
            dma((PIECES, 2)),
            dma((PIECES, 2)),
            dma((PIECES, 2)),
            dma((PIECES,)),
            dma((3,)),
            dma((ADAM_PARTS, 4)),
            dma((PIECES + 1,)),
        ],
        compiler_params=pltpu.CompilerParams(collective_id=0, has_side_effects=True, vmem_limit_bytes=40 << 20),
    )(
        *placed(pltpu.HBM, tokens), norm_gain.reshape(1, width),
        *placed(pltpu.HBM, lengths, queries, key_cache, value_cache, master, moment_first, moment_second, gradient),
    )
    return pl.pallas_call(
        write_kernel,
        out_shape=tuple(jax.ShapeDtypeStruct(result.shape, result.dtype) for result in results),
        in_specs=[vmem] * len(results),
        out_specs=(anywhere,) * len(results),
        scratch_shapes=[dma((len(results),))],
        compiler_params=pltpu.CompilerParams(vmem_limit_bytes=4 << 20),
    )(*placed(pltpu.VMEM, *results))


def fits(sizes, tokens, master, queries, key_cache):
    grp, tp, fs = sizes
    batch_rows, steps, width = tokens.shape
    rows, depth, columns = batch_rows * steps, master.shape[0], master.shape[1]
    slots, kv_width = key_cache.shape[1:]
    if tp != 2 or fs != 2 or grp != 2 * tp * fs or width != 2 * depth or 128 % slots or slots % 16:
        return False
    few = 128 // slots
    return (
        depth % (32 * ADAM_PARTS) == 0 and depth % 128 == 0 and rows % 128 == 0 and rows % (16 * PIECES) == 0
        and columns == 2 * kv_width and few * steps % 16 == 0 and batch_rows % (few * PIECES) == 0
        and queries.shape[2] % kv_width == 0
    )


def project_gathered(tokens, norm_gain, layer_half):
    batch_rows, steps = (tokens.shape[0], tokens.shape[1])
    widened, gain_whole = (
        lax.all_gather(tokens, ("tp", "fs"), axis=2, tiled=True),
        lax.all_gather(norm_gain, ("tp", "fs"), axis=0, tiled=True),
    )
    mean_square = (
        jnp.einsum("rsd,rsd->rs", widened, widened, preferred_element_type=jnp.float32)[..., None]
        / MODEL_WIDTH
    )
    normed = (widened * lax.rsqrt(mean_square + norm_eps) * gain_whole.astype(jnp.float32)).astype(
        jnp.bfloat16
    )
    flattened = normed.reshape(batch_rows * steps, MODEL_WIDTH)
    gathered = lax.all_gather(layer_half, "grp", axis=0, tiled=True)
    return jnp.dot(flattened, gathered, preferred_element_type=jnp.float32)


def shards(
    sizes,
    tokens,
    norm_gain,
    queries,
    rotated_key_cache,
    head_value_cache,
    lengths,
    master,
    moment_first,
    moment_second,
    gradient,
):
    if fits(sizes, tokens, master, queries, rotated_key_cache):
        return project_and_attend(
            sizes, tokens, norm_gain, queries, rotated_key_cache, head_value_cache, lengths, master, moment_first, moment_second,
            gradient,
        )
    average = beta_first * moment_first + (1.0 - beta_first) * gradient
    variance = beta_second * moment_second + (1.0 - beta_second) * gradient * gradient
    update = average / correct_first / (jnp.sqrt(variance / correct_second) + adam_eps)
    renewed = master - learn_rate * (update + decay_rate * master)
    layer_half = renewed.astype(jnp.bfloat16)
    batch_rows, steps = (tokens.shape[0], tokens.shape[1])
    columns = layer_half.shape[1]
    projected_output = project_gathered(tokens, norm_gain, layer_half)
    kv_heads = columns // (2 * HEAD_SIZE)
    projected_output = projected_output.reshape(batch_rows, steps, kv_heads, 2, HEAD_SIZE)
    positions = (lengths[:, None] + jnp.arange(steps, dtype=jnp.int32)[None, :]).astype(jnp.float32)
    key_new = rotate(projected_output[:, :, :, 0, :], positions).astype(jnp.bfloat16)
    value_new = projected_output[:, :, :, 1, :].astype(jnp.bfloat16)
    appended = jnp.stack([key_new, value_new], axis=3).reshape(batch_rows, steps, columns)
    attended = attention(queries, rotated_key_cache, head_value_cache, key_new, value_new, lengths)
    return (attended, appended, renewed, average, variance)


def solution(mesh):
    in_specs = (
        P("grp", None, ("tp", "fs")),
        P(("tp", "fs")),
        P("grp", None, ("tp", "fs")),
        P("grp", None, ("tp", "fs")),
        P("grp", None, ("tp", "fs")),
        P("grp"),
        P("grp", ("tp", "fs")),
        P("grp", ("tp", "fs")),
        P("grp", ("tp", "fs")),
        P("grp", ("tp", "fs")),
    )
    out_specs = (
        P("grp", None, ("tp", "fs")),
        P("grp", None, ("tp", "fs")),
        P("grp", ("tp", "fs")),
        P("grp", ("tp", "fs")),
        P("grp", ("tp", "fs")),
    )
    return jax.shard_map(
        functools.partial(shards, tuple(mesh.shape[name] for name in ("grp", "tp", "fs"))), mesh=mesh, in_specs=in_specs, out_specs=out_specs, check_vma=False,
    )
```

```python
import functools
import math

import jax
import jax.numpy as jnp
from jax import lax
from jax.experimental import pallas as pl
from jax.experimental.pallas import tpu as pltpu
from jax.sharding import PartitionSpec as P

MESH_ID = pl.DeviceIdType.MESH
PIECES = 4
ADAM_PARTS = 8
AHEAD = 2
LEAD = 5
NEXT = 1
LAG = 3
LAG_GATE = 3

MODEL_WIDTH = 8192
QUERY_HEADS = 64
KEY_VALUE_HEADS = 8
HEAD_SIZE = 128


beta_first = 0.9
beta_second = 0.999
correct_first = 0.9999734386011124
correct_second = 0.09520785288629038
adam_eps = 1e-08
learn_rate = 0.003
decay_rate = 0.1
norm_eps = 1e-06
rope_base = 1000000.0


def rotate(keys, positions):
    halfway = keys.shape[-1] // 2
    frequency = rope_base ** (-(jnp.arange(halfway, dtype=jnp.float32) * 2.0 / keys.shape[-1]))
    angles = positions[:, :, None] * frequency[None, None, :]
    cosine = jnp.cos(angles)[:, :, None, :]
    sine = jnp.sin(angles)[:, :, None, :]
    first_half = keys[..., :halfway]
    second_half = keys[..., halfway:]
    return jnp.concatenate(
        [first_half * cosine - second_half * sine, second_half * cosine + first_half * sine],
        axis=-1,
    )


def attention(queries, rotated_key_cache, head_value_cache, key_new, value_new, lengths):
    batch_rows, steps = (queries.shape[0], queries.shape[1])
    window = rotated_key_cache.shape[1]
    kv_heads = rotated_key_cache.shape[2] // HEAD_SIZE
    sharing_factor = QUERY_HEADS // KEY_VALUE_HEADS
    factor = HEAD_SIZE ** (-0.5)
    query_heads = queries.reshape(batch_rows, steps, kv_heads, sharing_factor, HEAD_SIZE)
    cache_key_seeds = rotated_key_cache.reshape(batch_rows, window, kv_heads, HEAD_SIZE)
    cache_values = head_value_cache.reshape(batch_rows, window, kv_heads, HEAD_SIZE)
    scores_cached = (
        jnp.einsum(
            "rsxgd,rlxd->rxgsl", query_heads, cache_key_seeds, preferred_element_type=jnp.float32
        )
        * factor
    )
    scores_fresh = (
        jnp.einsum("rsxgd,ruxd->rxgsu", query_heads, key_new, preferred_element_type=jnp.float32)
        * factor
    )
    present = (jnp.arange(window, dtype=jnp.int32)[None, :] < lengths[:, None])[
        :, None, None, None, :
    ]
    causal = (
        jnp.arange(steps, dtype=jnp.int32)[None, :] <= jnp.arange(steps, dtype=jnp.int32)[:, None]
    )[None, None, None, :, :]
    scores_cached = jnp.where(present, scores_cached, -jnp.inf)
    scores_fresh = jnp.where(causal, scores_fresh, -jnp.inf)
    ceiling = jnp.maximum(
        jnp.max(scores_cached, axis=-1, keepdims=True),
        jnp.max(scores_fresh, axis=-1, keepdims=True),
    )
    probs_cached = jnp.exp(scores_cached - ceiling)
    probs_fresh = jnp.exp(scores_fresh - ceiling)
    denom = jnp.sum(probs_cached, axis=-1, keepdims=True) + jnp.sum(
        probs_fresh, axis=-1, keepdims=True
    )
    weights_cached = probs_cached.astype(jnp.bfloat16)
    weights_fresh = probs_fresh.astype(jnp.bfloat16)
    blended = jnp.einsum(
        "rxgsl,rlxd->rsxgd", weights_cached, cache_values, preferred_element_type=jnp.float32
    )
    blended = blended + jnp.einsum(
        "rxgsu,ruxd->rsxgd", weights_fresh, value_new, preferred_element_type=jnp.float32
    )
    blended = blended / jnp.transpose(denom, (0, 3, 1, 2, 4))
    return blended.astype(jnp.bfloat16).reshape(
        batch_rows, steps, kv_heads * sharing_factor * HEAD_SIZE
    )


def exchange_kernel(sizes, tok_hbm, gain_hbm, len_ref, q_hbm, k_hbm, v_hbm, mas_hbm, fir_hbm, sec_hbm, gra_hbm, out_ref,
                    new_ref, mas_ref, fir_ref, sec_ref, tok_ref, gain_ref, cos_ref, sin_ref, present_ref, app_ref, gra_ref, w_ref,
                    sent, transit, held, squares, squares_in, scale_ref, total, pair_out, pair_in, near_out, near_in, mid_out,
                    mid_in, far_out, far_in, q_ref, k_ref, v_ref, part_out, part_max, part_sum, sq_s, sq_r, tok_s, tok_r, tr_r,
                    rl_s, fx_s, fc_s, pair_s, pair_r, near_s, near_r, mid_s, mid_r, far_s, far_r, load_s, adam_s, first_s):
    grp, tp, fs = sizes
    line = grp // 2
    g, t, f = lax.axis_index("grp"), lax.axis_index("tp"), lax.axis_index("fs")
    z, y = g // 2, lax.rem(g, 2)
    batch_rows, steps, width = tok_ref.shape
    rows = batch_rows * steps
    depth = w_ref.shape[0]
    blocks = width // depth
    piece = rows // PIECES
    lot = batch_rows // PIECES
    me = t * fs + f
    owner_t, owner_f = z // fs, lax.rem(z, fs)
    half_z, side = z // 2, lax.rem(z, 2)
    near = half_z * 2 + 1 - side
    gate = side != half_z
    far_gate = 2 - half_z
    far_outer = 3 * (1 - half_z)
    zs_of = (z, near, far_gate, far_outer)

    def remote(src, dst, ss, rs, device):
        return pltpu.make_async_remote_copy(
            src_ref=src, dst_ref=dst, send_sem=ss, recv_sem=rs, device_id=device, device_id_type=MESH_ID
        )

    barrier = pltpu.get_barrier_semaphore()
    mates = [(g, 1 - t, f), (g, t, 1 - f), (g, 1 - t, 1 - f)]
    peers = [(lax.rem(g + i, grp), t, k) for i in range(1, grp) for k in (f, 1 - f)]
    loads = [
        pltpu.make_async_copy(src, dst, load_s.at[i])
        for i, (src, dst) in enumerate(((q_hbm, q_ref), (k_hbm, k_ref), (v_hbm, v_ref)))
    ]
    part_rows = depth // ADAM_PARTS
    adam_loads = [
        [
            pltpu.make_async_copy(src.at[pl.ds(a * part_rows, part_rows)], dst.at[pl.ds(a * part_rows, part_rows)], adam_s.at[a, i])
            for i, (src, dst) in enumerate(((mas_hbm, mas_ref), (fir_hbm, fir_ref), (sec_hbm, sec_ref), (gra_hbm, gra_ref)))
        ]
        for a in range(ADAM_PARTS)
    ]
    first = [pltpu.make_async_copy(gain_hbm, gain_ref, first_s.at[PIECES])] + [
        pltpu.make_async_copy(tok_hbm.at[pl.ds(c * lot, lot)], tok_ref.at[pl.ds(c * lot, lot)], first_s.at[c])
        for c in range(PIECES)
    ]
    for copy in first:
        copy.start()
    for device in peers + mates:
        pl.semaphore_signal(barrier, inc=1, device_id=device, device_id_type=MESH_ID)
    for copies in adam_loads:
        for copy in copies:
            copy.start()
    for copy in loads:
        copy.start()

    def tokens_of(c, cols):
        return tok_ref[pl.ds(c * lot, lot), :, cols].reshape(piece, cols.size).astype(jnp.float32)

    def fill(c):
        for copy in first[: 2] if c == 0 else first[c + 1 : c + 2]:
            copy.wait()
        for j in range(blocks):
            cols = pl.ds(j * depth, depth)
            gain = gain_ref[cols].astype(jnp.float32).reshape(1, depth)
            sent[c, j] = (tokens_of(c, cols) * gain).astype(jnp.bfloat16)

    def send(c, end):
        for turn in range(2):
            j = lax.rem(y + c + turn, 2)
            dest = me * blocks + j
            src = sent.at[c, j]
            away = remote(src, held.at[c, g], tok_s.at[c, turn], tok_r.at[c, g], (dest, t, f))
            cross = remote(src, transit.at[c], tok_s.at[c, turn], tr_r.at[c], mates[1])
            direct = (dest != g) if turn == 0 else (dest != g) & (me == z)

            @pl.when(direct)
            def _():
                away.wait_send() if end else away.start()

            if turn == 1:

                @pl.when(me != z)
                def _():
                    cross.wait_send() if end else cross.start()

            if not end:

                @pl.when(dest == g)
                def _():
                    pltpu.make_async_copy(src, held.at[c, g], tok_r.at[c, g]).start()

    other = t * fs + 1 - f

    def relay(c, end):
        j = lax.rem(y + c + 1, 2)
        copy = remote(transit.at[c], held.at[c, g], rl_s.at[c], tok_r.at[c, g], (other * blocks + j, t, f))

        @pl.when(other != z)
        def _():
            if end:
                copy.wait_send()
            else:
                remote(transit.at[c], transit.at[c], rl_s.at[c], tr_r.at[c], mates[1]).wait_recv()
                copy.start()

    def slot_copies(c, i, turn):
        slot = zs_of[i] * 2 + lax.rem(y + c + turn, 2)
        first_f = owner_f if i == 0 or turn == 0 else 1 - owner_f
        block = held.at[c, slot]
        across = remote(block, block, fx_s.at[c, 2 * i + turn], tok_r.at[c, slot], mates[1])
        beside = remote(block, block, fc_s.at[c, 2 * i + turn], tok_r.at[c, slot], mates[0])
        return across, beside, first_f

    def lead(c, i):
        for turn in range(2):
            across, beside, first_f = slot_copies(c, i, turn)

            @pl.when((t == owner_t) & (f == first_f))
            def _():
                across.wait_recv()
                across.start()
                beside.start()

    def second(c, i):
        for turn in range(2):
            across, beside, first_f = slot_copies(c, i, turn)

            @pl.when((t == owner_t) & (f != first_f))
            def _():
                across.wait_recv()
                beside.start()

    def third(c, i):
        for turn in range(2):
            across, _, _ = slot_copies(c, i, turn)

            @pl.when(t != owner_t)
            def _():
                across.wait_recv()

    def sent_on(c, i):
        for turn in range(2):
            across, beside, first_f = slot_copies(c, i, turn)

            @pl.when((t == owner_t) & (f == first_f))
            def _():
                across.wait_send()

            @pl.when(t == owner_t)
            def _():
                beside.wait_send()

    def adam(a):
        for copy in adam_loads[a]:
            copy.wait()
        few_rows = 32

        def body(r, carry):
            window = pl.ds(pl.multiple_of(a * part_rows + r * few_rows, few_rows), few_rows)
            slope, old = gra_ref[window, :], mas_ref[window, :]
            average = beta_first * fir_ref[window, :] + (1.0 - beta_first) * slope
            variance = beta_second * sec_ref[window, :] + (1.0 - beta_second) * slope * slope
            update = average / correct_first / (jnp.sqrt(variance / correct_second) + adam_eps)
            renewed = old - learn_rate * (update + decay_rate * old)
            fir_ref[window, :] = average
            sec_ref[window, :] = variance
            mas_ref[window, :] = renewed
            w_ref[window, :] = renewed.astype(jnp.bfloat16)
            return carry

        lax.fori_loop(0, part_rows // few_rows, body, 0)

    sq = [remote(squares, squares_in.at[i], sq_s.at[i], sq_r.at[i], mates[i]) for i in range(3)]

    def start_squares():
        for c in range(PIECES):
            wide = tokens_of(c, pl.ds(0, width))
            wide = wide * wide
            part = wide[:, :128]
            for i in range(1, width // 128):
                part = part + wide[:, i * 128 : (i + 1) * 128]
            scale_ref[pl.ds(c * piece, piece), :] = part
        squares[...] = jnp.broadcast_to(jnp.sum(scale_ref[...].T, axis=0, keepdims=True), squares.shape)
        for copy in sq:
            copy.start()

    def finish_squares():
        for copy in sq:
            copy.wait()
        summed = (squares[...] + squares_in[0]) + (squares_in[1] + squares_in[2])
        scale = lax.rsqrt(summed / (width * tp * fs) + norm_eps)
        scale_ref[...] = jnp.broadcast_to(scale[0:1], (128, rows)).T

    def pair_copy(c, i):
        return remote(pair_out.at[c, i], pair_in.at[c, i], pair_s.at[c, i], pair_r.at[c, i], (z * 2 + 1 - y, t, f))

    def near_copy(c):
        return remote(near_out.at[c], near_in.at[c], near_s.at[c], near_r.at[c], (near * 2 + y, t, f))

    def mid_copy(c, k):
        return remote(mid_out.at[c, k], mid_in.at[c, k], mid_s.at[c, k], mid_r.at[c, k], (near * 2 + y, t, f))

    def far_copy(c, k):
        return remote(far_out.at[c, k], far_in.at[c], far_s.at[c, k], far_r.at[c], (zs_of[2 + k] * 2 + y, t, f))

    def multiply(c, i):
        slots2 = held[c, pl.ds(zs_of[i] * 2, 2)].reshape(2 * piece, depth)
        product = jnp.dot(slots2, w_ref[...], preferred_element_type=jnp.float32)
        total[c, i] = product.reshape(2, piece, product.shape[1])
        pair_out[c, i] = total[c, i, 1 - y].astype(jnp.bfloat16)
        pair_copy(c, i).start()

    def combine(c, i):
        pair_copy(c, i).wait_recv()
        both = total[c, i, y] + pair_in[c, i].astype(jnp.float32)
        if i == 0:
            total[c, 0, 0] = both
        elif i == 1:
            near_out[c] = both.astype(jnp.bfloat16)
            near_copy(c).start()
        else:

            @pl.when(gate)
            def _():
                total[c, i, 0] = both

            @pl.when(jnp.logical_not(gate))
            def _():
                mid_out[c, i - 2] = both.astype(jnp.bfloat16)
                mid_copy(c, i - 2).start()

    def pass_on(c, i):
        if i >= 2:

            @pl.when(gate)
            def _():
                mid_copy(c, i - 2).wait_recv()
                far_out[c, i - 2] = (total[c, i, 0] + mid_in[c, i - 2].astype(jnp.float32)).astype(jnp.bfloat16)
                far_copy(c, i - 2).start()

    _, slots, kv_width = k_ref.shape
    kv_heads = kv_width // HEAD_SIZE
    share = q_ref.shape[2] // kv_width
    few = 128 // slots
    band = few * steps
    factor = HEAD_SIZE ** (-0.5)
    chunks = batch_rows // few
    over_last = (((1,), (1,)), ((), ()))

    def head_lanes(x, h):
        return pl.ds((x * share + h) * HEAD_SIZE, HEAD_SIZE)

    def some_queries(b, x):
        return jnp.concatenate(
            [q_ref[pl.ds(b * few, few), :, head_lanes(x, h)].reshape(band, HEAD_SIZE) for h in range(share)], axis=0
        )

    def attend_cached(b):
        shape = (share * band, few * slots)
        row = lax.rem(lax.broadcasted_iota(jnp.int32, shape, 0), band) // steps
        same = row == lax.broadcasted_iota(jnp.int32, shape, 1) // slots
        valid = same & (present_ref[pl.ds(b, 1), :] > 0.5)
        for x in range(kv_heads):
            lanes = pl.ds(x * HEAD_SIZE, HEAD_SIZE)
            keys = k_ref[pl.ds(b * few, few), :, lanes].reshape(few * slots, HEAD_SIZE)
            values = v_ref[pl.ds(b * few, few), :, lanes].reshape(few * slots, HEAD_SIZE)
            scores = (
                lax.dot_general(some_queries(b, x), keys, over_last, preferred_element_type=jnp.float32) * factor
            )
            scores = jnp.where(valid, scores, -jnp.inf)
            most = jnp.max(scores, axis=1, keepdims=True)
            probs = jnp.exp(scores - most)
            part_max[b, x] = jnp.broadcast_to(most, (share * band, HEAD_SIZE))
            part_sum[b, x] = jnp.broadcast_to(jnp.sum(probs, axis=1, keepdims=True), (share * band, HEAD_SIZE))
            part_out[b, x] = jnp.dot(probs.astype(jnp.bfloat16), values, preferred_element_type=jnp.float32)

    def attend_new(b):
        shape = (share * band, band)
        mine = lax.rem(lax.broadcasted_iota(jnp.int32, shape, 0), band)
        other_row = lax.broadcasted_iota(jnp.int32, shape, 1)
        valid = (mine // steps == other_row // steps) & (other_row <= mine)
        window = pl.ds(b * band, band)
        for x in range(kv_heads):
            keys = app_ref[window, pl.ds(2 * x * HEAD_SIZE, HEAD_SIZE)]
            values = app_ref[window, pl.ds((2 * x + 1) * HEAD_SIZE, HEAD_SIZE)]
            scores = (
                lax.dot_general(some_queries(b, x), keys, over_last, preferred_element_type=jnp.float32) * factor
            )
            scores = jnp.where(valid, scores, -jnp.inf)
            before = part_max[b, x]
            most = jnp.maximum(before, jnp.max(scores, axis=1, keepdims=True))
            probs = jnp.exp(scores - most[:, :1])
            again = jnp.exp(before - most)
            denom = again * part_sum[b, x] + jnp.sum(probs, axis=1, keepdims=True)
            blended = again * part_out[b, x] + jnp.dot(
                probs.astype(jnp.bfloat16), values, preferred_element_type=jnp.float32
            )
            blended = (blended / denom).astype(jnp.bfloat16)
            for h in range(share):
                out_ref[pl.ds(b * few, few), :, head_lanes(x, h)] = blended[h * band : (h + 1) * band].reshape(
                    few, steps, HEAD_SIZE
                )

    half = HEAD_SIZE // 2

    def prepare():
        lane = lax.broadcasted_iota(jnp.int32, (1, few * slots), 1)
        for b in range(chunks):
            lengths = jnp.full(lane.shape, len_ref[b * few], jnp.int32)
            for k in range(1, few):
                lengths = jnp.where(lane // slots == k, len_ref[b * few + k], lengths)
            present_ref[pl.ds(b, 1), :] = (lax.rem(lane, slots) < lengths).astype(jnp.float32)
        for b in range(batch_rows):
            cos_ref[pl.ds(b * steps, steps), :] = jnp.full((steps, HEAD_SIZE), len_ref[b].astype(jnp.float32))
        lane = lax.broadcasted_iota(jnp.int32, (8, HEAD_SIZE), 1)
        exponent = lax.rem(lane, half).astype(jnp.float32) * (2.0 / HEAD_SIZE)
        frequency = jnp.exp(exponent * (-math.log(rope_base)))
        sign = jnp.where(lane < half, -1.0, 1.0)
        step = lax.rem(lax.broadcasted_iota(jnp.int32, (8, HEAD_SIZE), 0), steps).astype(jnp.float32)

        def body(r, carry):
            window = pl.ds(pl.multiple_of(r * 8, 8), 8)
            angles = (cos_ref[window, :] + step) * frequency
            cos_ref[window, :] = jnp.cos(angles)
            sin_ref[window, :] = jnp.sin(angles) * sign
            return carry

        lax.fori_loop(0, rows // 8, body, 0)

    def finish(c):
        window = pl.ds(c * piece, piece)
        near_copy(c).wait_recv()
        far_copy(c, 0).wait_recv()
        scale = scale_ref[window, :]
        for x in range(kv_heads):
            lanes = pl.ds(2 * x * HEAD_SIZE, HEAD_SIZE)
            later = pl.ds((2 * x + 1) * HEAD_SIZE, HEAD_SIZE)

            def summed(cols):
                arrived = near_in[c, :, cols].astype(jnp.float32) + far_in[c, :, cols].astype(jnp.float32)
                return (total[c, 0, 0, :, cols] + arrived) * scale

            key = summed(lanes)
            key = key * cos_ref[window, :] + pltpu.roll(key, half, 1) * sin_ref[window, :]
            for cols, part in ((lanes, key), (later, summed(later))):
                part = part.astype(jnp.bfloat16)
                app_ref[window, cols] = part
                new_ref[pl.ds(c * lot, lot), :, cols] = part.reshape(lot, steps, HEAD_SIZE)
        for b in range(c * chunks // PIECES, (c + 1) * chunks // PIECES):
            attend_new(b)

    fill(0)
    pl.semaphore_wait(barrier, len(peers) + len(mates))
    send(0, False)
    for c in range(1, AHEAD):
        fill(c)
        send(c, False)
    for c in range(AHEAD, PIECES):
        fill(c)
    start_squares()
    prepare()

    order = [(c, i) for c in range(PIECES) for i in ((0, 1, 2, 3) if c == 0 else (2, 3, 1, 0))]
    count = len(order)

    def arrive(n):
        c, i = order[n]
        if n % line == 0:
            if c == 0:
                relay(0, False)
            if c + AHEAD < PIECES:
                send(c + AHEAD, False)
            if c + 1 < PIECES:
                relay(c + 1, False)
        lead(c, i)

    for n in range(LEAD):
        adam_until = (n + 1) * ADAM_PARTS // LEAD
        for a in range(n * ADAM_PARTS // LEAD, adam_until):
            adam(a)
        arrive(n)
        if n >= LEAD - NEXT:
            second(*order[n - LEAD + NEXT])
    finish_squares()
    for copy in loads:
        copy.wait()
    done = 0
    steps_now = -(-chunks // (count - 4))
    def drain(c):
        send(c, True)
        relay(c, True)
        for i in range(line):
            sent_on(c, i)
            pair_copy(c, i).wait_send()
        near_copy(c).wait_send()
        for k in range(2):

            @pl.when(gate)
            def _():
                far_copy(c, k).wait_send()

            @pl.when(jnp.logical_not(gate))
            def _():
                mid_copy(c, k).wait_send()

    def combine_range(start, stop):
        for m in range(max(start, 0), stop):
            combine(*order[m])

    def pass_range(start, stop):
        for m in range(max(start, 0), stop):
            pass_on(*order[m])
            if m % line == line - 1 and line <= m < count - 1:
                finish(m // line - 1)
                drain(m // line - 1)

    for n in range(count):
        if n + LEAD < count:
            arrive(n + LEAD)
        if n + NEXT < count:
            second(*order[n + NEXT])
        third(*order[n])
        multiply(*order[n])
        combine_range(n - LAG, n - LAG + 1)
        for b in range(done, min(done + steps_now, chunks)):
            attend_cached(b)
        done = min(done + steps_now, chunks)
        pass_range(n - LAG - LAG_GATE, n - LAG - LAG_GATE + 1)
    last = count - line
    combine_range(count - LAG, last + 3)
    pass_range(count - LAG - LAG_GATE, last + 2)
    combine_range(max(count - LAG, last + 3), count)
    finish(PIECES - 2)
    drain(PIECES - 2)
    finish(PIECES - 1)
    drain(PIECES - 1)


def write_kernel(*refs):
    count = len(refs) // 2
    copies = [pltpu.make_async_copy(refs[i], refs[count + i], refs[-1].at[i]) for i in range(count)]
    for copy in copies:
        copy.start()
    for copy in copies:
        copy.wait()


def project_and_attend(sizes, tokens, norm_gain, queries, key_cache, value_cache, lengths, master, moment_first, moment_second,
                       gradient):
    grp, _, _ = sizes
    batch_rows, steps, width = tokens.shape
    _, slots, kv_width = key_cache.shape
    rows = batch_rows * steps
    depth, columns = master.shape
    blocks, line = width // depth, grp // 2
    kv_heads, share = kv_width // HEAD_SIZE, queries.shape[2] // kv_width
    few = 128 // slots
    piece = rows // PIECES
    dma = pltpu.SemaphoreType.DMA
    vmem = pl.BlockSpec(memory_space=pltpu.VMEM)
    anywhere = pl.BlockSpec(memory_space=pltpu.HBM)
    smem = pl.BlockSpec(memory_space=pltpu.SMEM)
    part = pltpu.VMEM((batch_rows // few, kv_heads, share * few * steps, HEAD_SIZE), jnp.float32)
    state = pltpu.VMEM(master.shape, jnp.float32)

    def placed(space, *arrays):
        return [pltpu.with_memory_space_constraint(array, space) for array in arrays]

    def half_width(*lead):
        return pltpu.VMEM((PIECES, *lead, piece, columns), jnp.bfloat16)

    results = pl.pallas_call(
        functools.partial(exchange_kernel, sizes),
        out_shape=(
            pltpu.VMEM(queries.shape, jnp.bfloat16),
            pltpu.VMEM((batch_rows, steps, columns), jnp.bfloat16),
            state,
            state,
            state,
        ),
        in_specs=[anywhere] * 2 + [smem] + [anywhere] * 7,
        out_specs=(vmem,) * 5,
        scratch_shapes=[
            pltpu.VMEM(tokens.shape, jnp.bfloat16),
            pltpu.VMEM((width,), jnp.bfloat16),
            pltpu.VMEM((rows, HEAD_SIZE), jnp.float32),
            pltpu.VMEM((rows, HEAD_SIZE), jnp.float32),
            pltpu.VMEM((batch_rows // few, few * slots), jnp.float32),
            pltpu.VMEM((rows, columns), jnp.bfloat16),
            pltpu.VMEM(master.shape, jnp.float32),
            pltpu.VMEM(master.shape, jnp.bfloat16),
            pltpu.VMEM((PIECES, blocks, piece, depth), jnp.bfloat16),
            pltpu.VMEM((PIECES, piece, depth), jnp.bfloat16),
            pltpu.VMEM((PIECES, grp, piece, depth), jnp.bfloat16),
            pltpu.VMEM((8, rows), jnp.float32),
            pltpu.VMEM((3, 8, rows), jnp.float32),
            pltpu.VMEM((rows, 128), jnp.float32),
            pltpu.VMEM((PIECES, line, 2, piece, columns), jnp.float32),
            half_width(line),
            half_width(line),
            half_width(),
            half_width(),
            half_width(2),
            half_width(2),
            half_width(2),
            half_width(),
            pltpu.VMEM(queries.shape, jnp.bfloat16),
            pltpu.VMEM(key_cache.shape, jnp.bfloat16),
            pltpu.VMEM(value_cache.shape, jnp.bfloat16),
            part,
            part,
            part,
            dma((3,)),
            dma((3,)),
            dma((PIECES, 2)),
            dma((PIECES, grp)),
            dma((PIECES,)),
            dma((PIECES,)),
            dma((PIECES, grp)),
            dma((PIECES, grp)),
            dma((PIECES, line)),
            dma((PIECES, line)),
            dma((PIECES,)),
            dma((PIECES,)),
            dma((PIECES, 2)),
            dma((PIECES, 2)),
            dma((PIECES, 2)),
            dma((PIECES,)),
            dma((3,)),
            dma((ADAM_PARTS, 4)),
            dma((PIECES + 1,)),
        ],
        compiler_params=pltpu.CompilerParams(collective_id=0, has_side_effects=True, vmem_limit_bytes=40 << 20),
    )(
        *placed(pltpu.HBM, tokens, norm_gain, lengths, queries, key_cache, value_cache, master, moment_first, moment_second, gradient),
    )
    return pl.pallas_call(
        write_kernel,
        out_shape=tuple(jax.ShapeDtypeStruct(result.shape, result.dtype) for result in results),
        in_specs=[vmem] * len(results),
        out_specs=(anywhere,) * len(results),
        scratch_shapes=[dma((len(results),))],
        compiler_params=pltpu.CompilerParams(vmem_limit_bytes=4 << 20),
    )(*placed(pltpu.VMEM, *results))


def fits(sizes, tokens, master, queries, key_cache):
    grp, tp, fs = sizes
    batch_rows, steps, width = tokens.shape
    rows, depth, columns = batch_rows * steps, master.shape[0], master.shape[1]
    slots, kv_width = key_cache.shape[1:]
    if tp != 2 or fs != 2 or grp != 2 * tp * fs or width != 2 * depth or 128 % slots or slots % 16:
        return False
    few = 128 // slots
    return (
        depth % (32 * ADAM_PARTS) == 0 and depth % 128 == 0 and rows % 128 == 0 and rows % (16 * PIECES) == 0
        and columns == 2 * kv_width and few * steps % 16 == 0 and batch_rows % (few * PIECES) == 0
        and queries.shape[2] % kv_width == 0
    )


def project_gathered(tokens, norm_gain, layer_half):
    batch_rows, steps = (tokens.shape[0], tokens.shape[1])
    widened, gain_whole = (
        lax.all_gather(tokens, ("tp", "fs"), axis=2, tiled=True),
        lax.all_gather(norm_gain, ("tp", "fs"), axis=0, tiled=True),
    )
    mean_square = (
        jnp.einsum("rsd,rsd->rs", widened, widened, preferred_element_type=jnp.float32)[..., None]
        / MODEL_WIDTH
    )
    normed = (widened * lax.rsqrt(mean_square + norm_eps) * gain_whole.astype(jnp.float32)).astype(
        jnp.bfloat16
    )
    flattened = normed.reshape(batch_rows * steps, MODEL_WIDTH)
    gathered = lax.all_gather(layer_half, "grp", axis=0, tiled=True)
    return jnp.dot(flattened, gathered, preferred_element_type=jnp.float32)


def shards(
    sizes,
    tokens,
    norm_gain,
    queries,
    rotated_key_cache,
    head_value_cache,
    lengths,
    master,
    moment_first,
    moment_second,
    gradient,
):
    if fits(sizes, tokens, master, queries, rotated_key_cache):
        return project_and_attend(
            sizes, tokens, norm_gain, queries, rotated_key_cache, head_value_cache, lengths, master, moment_first, moment_second,
            gradient,
        )
    average = beta_first * moment_first + (1.0 - beta_first) * gradient
    variance = beta_second * moment_second + (1.0 - beta_second) * gradient * gradient
    update = average / correct_first / (jnp.sqrt(variance / correct_second) + adam_eps)
    renewed = master - learn_rate * (update + decay_rate * master)
    layer_half = renewed.astype(jnp.bfloat16)
    batch_rows, steps = (tokens.shape[0], tokens.shape[1])
    columns = layer_half.shape[1]
    projected_output = project_gathered(tokens, norm_gain, layer_half)
    kv_heads = columns // (2 * HEAD_SIZE)
    projected_output = projected_output.reshape(batch_rows, steps, kv_heads, 2, HEAD_SIZE)
    positions = (lengths[:, None] + jnp.arange(steps, dtype=jnp.int32)[None, :]).astype(jnp.float32)
    key_new = rotate(projected_output[:, :, :, 0, :], positions).astype(jnp.bfloat16)
    value_new = projected_output[:, :, :, 1, :].astype(jnp.bfloat16)
    appended = jnp.stack([key_new, value_new], axis=3).reshape(batch_rows, steps, columns)
    attended = attention(queries, rotated_key_cache, head_value_cache, key_new, value_new, lengths)
    return (attended, appended, renewed, average, variance)


def solution(mesh):
    in_specs = (
        P("grp", None, ("tp", "fs")),
        P(("tp", "fs")),
        P("grp", None, ("tp", "fs")),
        P("grp", None, ("tp", "fs")),
        P("grp", None, ("tp", "fs")),
        P("grp"),
        P("grp", ("tp", "fs")),
        P("grp", ("tp", "fs")),
        P("grp", ("tp", "fs")),
        P("grp", ("tp", "fs")),
    )
    out_specs = (
        P("grp", None, ("tp", "fs")),
        P("grp", None, ("tp", "fs")),
        P("grp", ("tp", "fs")),
        P("grp", ("tp", "fs")),
        P("grp", ("tp", "fs")),
    )
    return jax.shard_map(
        functools.partial(shards, tuple(mesh.shape[name] for name in ("grp", "tp", "fs"))), mesh=mesh, in_specs=in_specs, out_specs=out_specs, check_vma=False,
    )
```

```python
import functools
import math

import jax
import jax.numpy as jnp
from jax import lax
from jax.experimental import pallas as pl
from jax.experimental.pallas import tpu as pltpu
from jax.sharding import PartitionSpec as P

MESH_ID = pl.DeviceIdType.MESH
PIECES = 4
ADAM_PARTS = 8
AHEAD = 2
LEAD = 5
NEXT = 0
LAG = 3
LAG_GATE = 3

MODEL_WIDTH = 8192
QUERY_HEADS = 64
KEY_VALUE_HEADS = 8
HEAD_SIZE = 128


beta_first = 0.9
beta_second = 0.999
correct_first = 0.9999734386011124
correct_second = 0.09520785288629038
adam_eps = 1e-08
learn_rate = 0.003
decay_rate = 0.1
norm_eps = 1e-06
rope_base = 1000000.0


def rotate(keys, positions):
    halfway = keys.shape[-1] // 2
    frequency = rope_base ** (-(jnp.arange(halfway, dtype=jnp.float32) * 2.0 / keys.shape[-1]))
    angles = positions[:, :, None] * frequency[None, None, :]
    cosine = jnp.cos(angles)[:, :, None, :]
    sine = jnp.sin(angles)[:, :, None, :]
    first_half = keys[..., :halfway]
    second_half = keys[..., halfway:]
    return jnp.concatenate(
        [first_half * cosine - second_half * sine, second_half * cosine + first_half * sine],
        axis=-1,
    )


def attention(queries, rotated_key_cache, head_value_cache, key_new, value_new, lengths):
    batch_rows, steps = (queries.shape[0], queries.shape[1])
    window = rotated_key_cache.shape[1]
    kv_heads = rotated_key_cache.shape[2] // HEAD_SIZE
    sharing_factor = QUERY_HEADS // KEY_VALUE_HEADS
    factor = HEAD_SIZE ** (-0.5)
    query_heads = queries.reshape(batch_rows, steps, kv_heads, sharing_factor, HEAD_SIZE)
    cache_key_seeds = rotated_key_cache.reshape(batch_rows, window, kv_heads, HEAD_SIZE)
    cache_values = head_value_cache.reshape(batch_rows, window, kv_heads, HEAD_SIZE)
    scores_cached = (
        jnp.einsum(
            "rsxgd,rlxd->rxgsl", query_heads, cache_key_seeds, preferred_element_type=jnp.float32
        )
        * factor
    )
    scores_fresh = (
        jnp.einsum("rsxgd,ruxd->rxgsu", query_heads, key_new, preferred_element_type=jnp.float32)
        * factor
    )
    present = (jnp.arange(window, dtype=jnp.int32)[None, :] < lengths[:, None])[
        :, None, None, None, :
    ]
    causal = (
        jnp.arange(steps, dtype=jnp.int32)[None, :] <= jnp.arange(steps, dtype=jnp.int32)[:, None]
    )[None, None, None, :, :]
    scores_cached = jnp.where(present, scores_cached, -jnp.inf)
    scores_fresh = jnp.where(causal, scores_fresh, -jnp.inf)
    ceiling = jnp.maximum(
        jnp.max(scores_cached, axis=-1, keepdims=True),
        jnp.max(scores_fresh, axis=-1, keepdims=True),
    )
    probs_cached = jnp.exp(scores_cached - ceiling)
    probs_fresh = jnp.exp(scores_fresh - ceiling)
    denom = jnp.sum(probs_cached, axis=-1, keepdims=True) + jnp.sum(
        probs_fresh, axis=-1, keepdims=True
    )
    weights_cached = probs_cached.astype(jnp.bfloat16)
    weights_fresh = probs_fresh.astype(jnp.bfloat16)
    blended = jnp.einsum(
        "rxgsl,rlxd->rsxgd", weights_cached, cache_values, preferred_element_type=jnp.float32
    )
    blended = blended + jnp.einsum(
        "rxgsu,ruxd->rsxgd", weights_fresh, value_new, preferred_element_type=jnp.float32
    )
    blended = blended / jnp.transpose(denom, (0, 3, 1, 2, 4))
    return blended.astype(jnp.bfloat16).reshape(
        batch_rows, steps, kv_heads * sharing_factor * HEAD_SIZE
    )


def attend_new_rows(sizes, b, at, q_ref, app_ref, out_ref, part):
    few, steps, slots, share, kv_heads = sizes
    band = few * steps
    factor = HEAD_SIZE ** (-0.5)
    part_out, part_max, part_sum = part
    shape = (share * band, band)
    mine = lax.rem(lax.broadcasted_iota(jnp.int32, shape, 0), band)
    other_row = lax.broadcasted_iota(jnp.int32, shape, 1)
    valid = (mine // steps == other_row // steps) & (other_row <= mine)
    window = pl.ds(b * band, band)
    for x in range(kv_heads):
        lanes = [pl.ds((x * share + h) * HEAD_SIZE, HEAD_SIZE) for h in range(share)]
        keys = app_ref[window, pl.ds(2 * x * HEAD_SIZE, HEAD_SIZE)]
        values = app_ref[window, pl.ds((2 * x + 1) * HEAD_SIZE, HEAD_SIZE)]
        asked = jnp.concatenate([q_ref[pl.ds(b * few, few), :, cols].reshape(band, HEAD_SIZE) for cols in lanes], axis=0)
        scores = (
            lax.dot_general(asked, keys, (((1,), (1,)), ((), ())), preferred_element_type=jnp.float32) * factor
        )
        scores = jnp.where(valid, scores, -jnp.inf)
        before = part_max[x]
        most = jnp.maximum(before, jnp.max(scores, axis=1, keepdims=True))
        probs = jnp.exp(scores - most[:, :1])
        again = jnp.exp(before - most)
        denom = again * part_sum[x] + jnp.sum(probs, axis=1, keepdims=True)
        blended = again * part_out[x] + jnp.dot(probs.astype(jnp.bfloat16), values, preferred_element_type=jnp.float32)
        blended = (blended / denom).astype(jnp.bfloat16)
        for h in range(share):
            out_ref[pl.ds(at * few, few), :, lanes[h]] = blended[h * band : (h + 1) * band].reshape(few, steps, HEAD_SIZE)


def exchange_kernel(sizes, tok_hbm, gain_hbm, len_ref, q_hbm, k_hbm, v_hbm, mas_hbm, fir_hbm, sec_hbm, gra_hbm, out_ref,
                    new_ref, mas_ref, fir_ref, sec_ref, q_ref, app_ref, late_out, late_max, late_sum, tok_ref, gain_ref, cos_ref,
                    sin_ref, present_ref, gra_ref, w_ref,
                    sent, transit, held, squares, squares_in, scale_ref, total, pair_out, pair_in, near_out, near_in, mid_out,
                    mid_in, far_out, far_in, k_ref, v_ref, part_out, part_max, part_sum, sq_s, sq_r, tok_s, tok_r, tr_r,
                    rl_s, fx_s, fc_s, pair_s, pair_r, near_s, near_r, mid_s, mid_r, far_s, far_r, load_s, adam_s, first_s):
    grp, tp, fs = sizes
    line = grp // 2
    g, t, f = lax.axis_index("grp"), lax.axis_index("tp"), lax.axis_index("fs")
    z, y = g // 2, lax.rem(g, 2)
    batch_rows, steps, width = tok_ref.shape
    rows = batch_rows * steps
    depth = w_ref.shape[0]
    blocks = width // depth
    piece = rows // PIECES
    lot = batch_rows // PIECES
    me = t * fs + f
    owner_t, owner_f = z // fs, lax.rem(z, fs)
    half_z, side = z // 2, lax.rem(z, 2)
    near = half_z * 2 + 1 - side
    gate = side != half_z
    far_gate = 2 - half_z
    far_outer = 3 * (1 - half_z)
    zs_of = (z, near, far_gate, far_outer)

    def remote(src, dst, ss, rs, device):
        return pltpu.make_async_remote_copy(
            src_ref=src, dst_ref=dst, send_sem=ss, recv_sem=rs, device_id=device, device_id_type=MESH_ID
        )

    barrier = pltpu.get_barrier_semaphore()
    mates = [(g, 1 - t, f), (g, t, 1 - f), (g, 1 - t, 1 - f)]
    peers = [(lax.rem(g + i, grp), t, k) for i in range(1, grp) for k in (f, 1 - f)]
    loads = [
        pltpu.make_async_copy(src, dst, load_s.at[i])
        for i, (src, dst) in enumerate(((q_hbm, q_ref), (k_hbm, k_ref), (v_hbm, v_ref)))
    ]
    part_rows = depth // ADAM_PARTS
    adam_loads = [
        [
            pltpu.make_async_copy(src.at[pl.ds(a * part_rows, part_rows)], dst.at[pl.ds(a * part_rows, part_rows)], adam_s.at[a, i])
            for i, (src, dst) in enumerate(((mas_hbm, mas_ref), (fir_hbm, fir_ref), (sec_hbm, sec_ref), (gra_hbm, gra_ref)))
        ]
        for a in range(ADAM_PARTS)
    ]
    first = [pltpu.make_async_copy(gain_hbm, gain_ref, first_s.at[PIECES])] + [
        pltpu.make_async_copy(tok_hbm.at[pl.ds(c * lot, lot)], tok_ref.at[pl.ds(c * lot, lot)], first_s.at[c])
        for c in range(PIECES)
    ]
    for copy in first:
        copy.start()
    for device in peers + mates:
        pl.semaphore_signal(barrier, inc=1, device_id=device, device_id_type=MESH_ID)
    for copies in adam_loads:
        for copy in copies:
            copy.start()
    for copy in loads:
        copy.start()

    def tokens_of(c, cols):
        return tok_ref[pl.ds(c * lot, lot), :, cols].reshape(piece, cols.size).astype(jnp.float32)

    def fill(c):
        for copy in first[: 2] if c == 0 else first[c + 1 : c + 2]:
            copy.wait()
        for j in range(blocks):
            cols = pl.ds(j * depth, depth)
            gain = gain_ref[cols].astype(jnp.float32).reshape(1, depth)
            sent[c, j] = (tokens_of(c, cols) * gain).astype(jnp.bfloat16)

    def send(c, end):
        for turn in range(2):
            j = lax.rem(y + c + turn, 2)
            dest = me * blocks + j
            src = sent.at[c, j]
            away = remote(src, held.at[c, g], tok_s.at[c, turn], tok_r.at[c, g], (dest, t, f))
            cross = remote(src, transit.at[c], tok_s.at[c, turn], tr_r.at[c], mates[1])
            direct = (dest != g) if turn == 0 else (dest != g) & (me == z)

            @pl.when(direct)
            def _():
                away.wait_send() if end else away.start()

            if turn == 1:

                @pl.when(me != z)
                def _():
                    cross.wait_send() if end else cross.start()

            if not end:

                @pl.when(dest == g)
                def _():
                    pltpu.make_async_copy(src, held.at[c, g], tok_r.at[c, g]).start()

    other = t * fs + 1 - f

    def relay(c, end):
        j = lax.rem(y + c + 1, 2)
        copy = remote(transit.at[c], held.at[c, g], rl_s.at[c], tok_r.at[c, g], (other * blocks + j, t, f))

        @pl.when(other != z)
        def _():
            if end:
                copy.wait_send()
            else:
                remote(transit.at[c], transit.at[c], rl_s.at[c], tr_r.at[c], mates[1]).wait_recv()
                copy.start()

    def slot_copies(c, i, turn):
        slot = zs_of[i] * 2 + lax.rem(y + c + turn, 2)
        first_f = owner_f if i == 0 or turn == 0 else 1 - owner_f
        block = held.at[c, slot]
        across = remote(block, block, fx_s.at[c, 2 * i + turn], tok_r.at[c, slot], mates[1])
        beside = remote(block, block, fc_s.at[c, 2 * i + turn], tok_r.at[c, slot], mates[0])
        return across, beside, first_f

    def lead(c, i):
        for turn in range(2):
            across, beside, first_f = slot_copies(c, i, turn)

            @pl.when((t == owner_t) & (f == first_f))
            def _():
                across.wait_recv()
                across.start()
                beside.start()

    def second(c, i):
        for turn in range(2):
            across, beside, first_f = slot_copies(c, i, turn)

            @pl.when((t == owner_t) & (f != first_f))
            def _():
                across.wait_recv()
                beside.start()

    def third(c, i):
        for turn in range(2):
            across, _, _ = slot_copies(c, i, turn)

            @pl.when(t != owner_t)
            def _():
                across.wait_recv()

    def sent_on(c, i):
        for turn in range(2):
            across, beside, first_f = slot_copies(c, i, turn)

            @pl.when((t == owner_t) & (f == first_f))
            def _():
                across.wait_send()

            @pl.when(t == owner_t)
            def _():
                beside.wait_send()

    def adam(a):
        for copy in adam_loads[a]:
            copy.wait()
        few_rows = 32

        def body(r, carry):
            window = pl.ds(pl.multiple_of(a * part_rows + r * few_rows, few_rows), few_rows)
            slope, old = gra_ref[window, :], mas_ref[window, :]
            average = beta_first * fir_ref[window, :] + (1.0 - beta_first) * slope
            variance = beta_second * sec_ref[window, :] + (1.0 - beta_second) * slope * slope
            update = average / correct_first / (jnp.sqrt(variance / correct_second) + adam_eps)
            renewed = old - learn_rate * (update + decay_rate * old)
            fir_ref[window, :] = average
            sec_ref[window, :] = variance
            mas_ref[window, :] = renewed
            w_ref[window, :] = renewed.astype(jnp.bfloat16)
            return carry

        lax.fori_loop(0, part_rows // few_rows, body, 0)

    sq = [remote(squares, squares_in.at[i], sq_s.at[i], sq_r.at[i], mates[i]) for i in range(3)]

    def start_squares():
        for c in range(PIECES):
            wide = tokens_of(c, pl.ds(0, width))
            wide = wide * wide
            part = wide[:, :128]
            for i in range(1, width // 128):
                part = part + wide[:, i * 128 : (i + 1) * 128]
            scale_ref[pl.ds(c * piece, piece), :] = part
        squares[...] = jnp.broadcast_to(jnp.sum(scale_ref[...].T, axis=0, keepdims=True), squares.shape)
        for copy in sq:
            copy.start()

    def finish_squares():
        for copy in sq:
            copy.wait()
        summed = (squares[...] + squares_in[0]) + (squares_in[1] + squares_in[2])
        scale = lax.rsqrt(summed / (width * tp * fs) + norm_eps)
        scale_ref[...] = jnp.broadcast_to(scale[0:1], (128, rows)).T

    def pair_copy(c, i):
        return remote(pair_out.at[c, i], pair_in.at[c, i], pair_s.at[c, i], pair_r.at[c, i], (z * 2 + 1 - y, t, f))

    def near_copy(c):
        return remote(near_out.at[c], near_in.at[c], near_s.at[c], near_r.at[c], (near * 2 + y, t, f))

    def mid_copy(c, k):
        return remote(mid_out.at[c, k], mid_in.at[c, k], mid_s.at[c, k], mid_r.at[c, k], (near * 2 + y, t, f))

    def far_copy(c, k):
        return remote(far_out.at[c, k], far_in.at[c], far_s.at[c, k], far_r.at[c], (zs_of[2 + k] * 2 + y, t, f))

    def multiply(c, i):
        slots2 = held[c, pl.ds(zs_of[i] * 2, 2)].reshape(2 * piece, depth)
        product = jnp.dot(slots2, w_ref[...], preferred_element_type=jnp.float32)
        total[c, i] = product.reshape(2, piece, product.shape[1])
        pair_out[c, i] = total[c, i, 1 - y].astype(jnp.bfloat16)
        pair_copy(c, i).start()

    def combine(c, i):
        pair_copy(c, i).wait_recv()
        both = total[c, i, y] + pair_in[c, i].astype(jnp.float32)
        if i == 0:
            total[c, 0, 0] = both
        elif i == 1:
            near_out[c] = both.astype(jnp.bfloat16)
            near_copy(c).start()
        else:

            @pl.when(gate)
            def _():
                total[c, i, 0] = both

            @pl.when(jnp.logical_not(gate))
            def _():
                mid_out[c, i - 2] = both.astype(jnp.bfloat16)
                mid_copy(c, i - 2).start()

    def pass_on(c, i):
        if i >= 2:

            @pl.when(gate)
            def _():
                mid_copy(c, i - 2).wait_recv()
                far_out[c, i - 2] = (total[c, i, 0] + mid_in[c, i - 2].astype(jnp.float32)).astype(jnp.bfloat16)
                far_copy(c, i - 2).start()

    _, slots, kv_width = k_ref.shape
    kv_heads = kv_width // HEAD_SIZE
    share = q_ref.shape[2] // kv_width
    few = 128 // slots
    band = few * steps
    factor = HEAD_SIZE ** (-0.5)
    chunks = batch_rows // few
    over_last = (((1,), (1,)), ((), ()))

    def head_lanes(x, h):
        return pl.ds((x * share + h) * HEAD_SIZE, HEAD_SIZE)

    def some_queries(b, x):
        return jnp.concatenate(
            [q_ref[pl.ds(b * few, few), :, head_lanes(x, h)].reshape(band, HEAD_SIZE) for h in range(share)], axis=0
        )

    early = chunks - chunks // PIECES

    def parts_of(b):
        if b < early:
            return part_out.at[b], part_max.at[b], part_sum.at[b]
        return late_out.at[b - early], late_max.at[b - early], late_sum.at[b - early]

    def attend_cached(b):
        to_out, to_max, to_sum = parts_of(b)
        shape = (share * band, few * slots)
        row = lax.rem(lax.broadcasted_iota(jnp.int32, shape, 0), band) // steps
        same = row == lax.broadcasted_iota(jnp.int32, shape, 1) // slots
        valid = same & (present_ref[pl.ds(b, 1), :] > 0.5)
        for x in range(kv_heads):
            lanes = pl.ds(x * HEAD_SIZE, HEAD_SIZE)
            keys = k_ref[pl.ds(b * few, few), :, lanes].reshape(few * slots, HEAD_SIZE)
            values = v_ref[pl.ds(b * few, few), :, lanes].reshape(few * slots, HEAD_SIZE)
            scores = (
                lax.dot_general(some_queries(b, x), keys, over_last, preferred_element_type=jnp.float32) * factor
            )
            scores = jnp.where(valid, scores, -jnp.inf)
            most = jnp.max(scores, axis=1, keepdims=True)
            probs = jnp.exp(scores - most)
            to_max[x] = jnp.broadcast_to(most, (share * band, HEAD_SIZE))
            to_sum[x] = jnp.broadcast_to(jnp.sum(probs, axis=1, keepdims=True), (share * band, HEAD_SIZE))
            to_out[x] = jnp.dot(probs.astype(jnp.bfloat16), values, preferred_element_type=jnp.float32)

    def attend_new(b):
        attend_new_rows((few, steps, slots, share, kv_heads), b, b, q_ref, app_ref, out_ref, parts_of(b))

    half = HEAD_SIZE // 2

    def prepare():
        lane = lax.broadcasted_iota(jnp.int32, (1, few * slots), 1)
        for b in range(chunks):
            lengths = jnp.full(lane.shape, len_ref[b * few], jnp.int32)
            for k in range(1, few):
                lengths = jnp.where(lane // slots == k, len_ref[b * few + k], lengths)
            present_ref[pl.ds(b, 1), :] = (lax.rem(lane, slots) < lengths).astype(jnp.float32)
        for b in range(batch_rows):
            cos_ref[pl.ds(b * steps, steps), :] = jnp.full((steps, HEAD_SIZE), len_ref[b].astype(jnp.float32))
        lane = lax.broadcasted_iota(jnp.int32, (8, HEAD_SIZE), 1)
        exponent = lax.rem(lane, half).astype(jnp.float32) * (2.0 / HEAD_SIZE)
        frequency = jnp.exp(exponent * (-math.log(rope_base)))
        sign = jnp.where(lane < half, -1.0, 1.0)
        step = lax.rem(lax.broadcasted_iota(jnp.int32, (8, HEAD_SIZE), 0), steps).astype(jnp.float32)

        def body(r, carry):
            window = pl.ds(pl.multiple_of(r * 8, 8), 8)
            angles = (cos_ref[window, :] + step) * frequency
            cos_ref[window, :] = jnp.cos(angles)
            sin_ref[window, :] = jnp.sin(angles) * sign
            return carry

        lax.fori_loop(0, rows // 8, body, 0)

    def finish(c):
        window = pl.ds(c * piece, piece)
        near_copy(c).wait_recv()
        far_copy(c, 0).wait_recv()
        scale = scale_ref[window, :]
        for x in range(kv_heads):
            lanes = pl.ds(2 * x * HEAD_SIZE, HEAD_SIZE)
            later = pl.ds((2 * x + 1) * HEAD_SIZE, HEAD_SIZE)

            def summed(cols):
                arrived = near_in[c, :, cols].astype(jnp.float32) + far_in[c, :, cols].astype(jnp.float32)
                return (total[c, 0, 0, :, cols] + arrived) * scale

            key = summed(lanes)
            key = key * cos_ref[window, :] + pltpu.roll(key, half, 1) * sin_ref[window, :]
            for cols, part in ((lanes, key), (later, summed(later))):
                part = part.astype(jnp.bfloat16)
                app_ref[window, cols] = part
                new_ref[pl.ds(c * lot, lot), :, cols] = part.reshape(lot, steps, HEAD_SIZE)
        for b in range(c * chunks // PIECES, min((c + 1) * chunks // PIECES, early)):
            attend_new(b)

    fill(0)
    pl.semaphore_wait(barrier, len(peers) + len(mates))
    send(0, False)
    for c in range(1, AHEAD):
        fill(c)
        send(c, False)
    for c in range(AHEAD, PIECES):
        fill(c)
    start_squares()
    prepare()

    order = [(c, i) for c in range(PIECES) for i in ((0, 1, 2, 3) if c == 0 else (2, 3, 1, 0))]
    count = len(order)

    def arrive(n):
        c, i = order[n]
        if n % line == 0:
            if c == 0:
                relay(0, False)
            if c + AHEAD < PIECES:
                send(c + AHEAD, False)
            if c + 1 < PIECES:
                relay(c + 1, False)
        lead(c, i)

    for n in range(LEAD):
        adam_until = (n + 1) * ADAM_PARTS // LEAD
        for a in range(n * ADAM_PARTS // LEAD, adam_until):
            adam(a)
        arrive(n)
        if n >= LEAD - NEXT:
            second(*order[n - LEAD + NEXT])
    finish_squares()
    for copy in loads:
        copy.wait()
    done = 0
    steps_now = -(-chunks // (count - 4))
    def drain(c):
        send(c, True)
        relay(c, True)
        for i in range(line):
            sent_on(c, i)
            pair_copy(c, i).wait_send()
        near_copy(c).wait_send()
        for k in range(2):

            @pl.when(gate)
            def _():
                far_copy(c, k).wait_send()

            @pl.when(jnp.logical_not(gate))
            def _():
                mid_copy(c, k).wait_send()

    def combine_range(start, stop):
        for m in range(max(start, 0), stop):
            combine(*order[m])

    def pass_range(start, stop):
        for m in range(max(start, 0), stop):
            pass_on(*order[m])
            if m % line == line - 1 and line <= m < count - 1:
                finish(m // line - 1)
                drain(m // line - 1)

    for n in range(count):
        if n + LEAD < count:
            arrive(n + LEAD)
        if n + NEXT < count:
            second(*order[n + NEXT])
        third(*order[n])
        multiply(*order[n])
        combine_range(n - LAG, n - LAG + 1)
        for b in range(done, min(done + steps_now, chunks)):
            attend_cached(b)
        done = min(done + steps_now, chunks)
        pass_range(n - LAG - LAG_GATE, n - LAG - LAG_GATE + 1)
    last = count - line
    combine_range(count - LAG, last + 3)
    pass_range(count - LAG - LAG_GATE, last + 2)
    combine_range(max(count - LAG, last + 3), count)
    finish(PIECES - 2)
    drain(PIECES - 2)
    finish(PIECES - 1)
    drain(PIECES - 1)


def write_kernel(sizes, att_ref, new_ref, mas_ref, fir_ref, sec_ref, q_ref, app_ref, late_out, late_max, late_sum, att_hbm,
                 new_hbm, mas_hbm, fir_hbm, sec_hbm, tail_ref, write_s):
    few = sizes[0]
    late = late_out.shape[0]
    early = att_ref.shape[0] // few - late
    first = pl.ds(0, early * few)
    moves = ((mas_ref, mas_hbm), (fir_ref, fir_hbm), (sec_ref, sec_hbm), (new_ref, new_hbm), (att_ref.at[first], att_hbm.at[first]))
    copies = [pltpu.make_async_copy(src, dst, write_s.at[i]) for i, (src, dst) in enumerate(moves)]
    for copy in copies:
        copy.start()
    for b in range(late):
        attend_new_rows(
            sizes, early + b, b, q_ref, app_ref, tail_ref, (late_out.at[b], late_max.at[b], late_sum.at[b])
        )
    copies.append(pltpu.make_async_copy(tail_ref, att_hbm.at[pl.ds(early * few, late * few)], write_s.at[len(moves)]))
    copies[-1].start()
    for copy in copies:
        copy.wait()


def project_and_attend(sizes, tokens, norm_gain, queries, key_cache, value_cache, lengths, master, moment_first, moment_second,
                       gradient):
    grp, _, _ = sizes
    batch_rows, steps, width = tokens.shape
    _, slots, kv_width = key_cache.shape
    rows = batch_rows * steps
    depth, columns = master.shape
    blocks, line = width // depth, grp // 2
    kv_heads, share = kv_width // HEAD_SIZE, queries.shape[2] // kv_width
    few = 128 // slots
    piece = rows // PIECES
    dma = pltpu.SemaphoreType.DMA
    vmem = pl.BlockSpec(memory_space=pltpu.VMEM)
    anywhere = pl.BlockSpec(memory_space=pltpu.HBM)
    smem = pl.BlockSpec(memory_space=pltpu.SMEM)
    chunks, block = batch_rows // few, (kv_heads, share * few * steps, HEAD_SIZE)
    late = pltpu.VMEM((chunks // PIECES, *block), jnp.float32)
    part = pltpu.VMEM((chunks - chunks // PIECES, *block), jnp.float32)
    state = pltpu.VMEM(master.shape, jnp.float32)

    def placed(space, *arrays):
        return [pltpu.with_memory_space_constraint(array, space) for array in arrays]

    def half_width(*lead):
        return pltpu.VMEM((PIECES, *lead, piece, columns), jnp.bfloat16)

    results = pl.pallas_call(
        functools.partial(exchange_kernel, sizes),
        out_shape=(
            pltpu.VMEM(queries.shape, jnp.bfloat16),
            pltpu.VMEM((batch_rows, steps, columns), jnp.bfloat16),
            state,
            state,
            state,
            pltpu.VMEM(queries.shape, jnp.bfloat16),
            pltpu.VMEM((rows, columns), jnp.bfloat16),
            late,
            late,
            late,
        ),
        in_specs=[anywhere] * 2 + [smem] + [anywhere] * 7,
        out_specs=(vmem,) * 10,
        scratch_shapes=[
            pltpu.VMEM(tokens.shape, jnp.bfloat16),
            pltpu.VMEM((width,), jnp.bfloat16),
            pltpu.VMEM((rows, HEAD_SIZE), jnp.float32),
            pltpu.VMEM((rows, HEAD_SIZE), jnp.float32),
            pltpu.VMEM((batch_rows // few, few * slots), jnp.float32),
            pltpu.VMEM(master.shape, jnp.float32),
            pltpu.VMEM(master.shape, jnp.bfloat16),
            pltpu.VMEM((PIECES, blocks, piece, depth), jnp.bfloat16),
            pltpu.VMEM((PIECES, piece, depth), jnp.bfloat16),
            pltpu.VMEM((PIECES, grp, piece, depth), jnp.bfloat16),
            pltpu.VMEM((8, rows), jnp.float32),
            pltpu.VMEM((3, 8, rows), jnp.float32),
            pltpu.VMEM((rows, 128), jnp.float32),
            pltpu.VMEM((PIECES, line, 2, piece, columns), jnp.float32),
            half_width(line),
            half_width(line),
            half_width(),
            half_width(),
            half_width(2),
            half_width(2),
            half_width(2),
            half_width(),
            pltpu.VMEM(key_cache.shape, jnp.bfloat16),
            pltpu.VMEM(value_cache.shape, jnp.bfloat16),
            part,
            part,
            part,
            dma((3,)),
            dma((3,)),
            dma((PIECES, 2)),
            dma((PIECES, grp)),
            dma((PIECES,)),
            dma((PIECES,)),
            dma((PIECES, grp)),
            dma((PIECES, grp)),
            dma((PIECES, line)),
            dma((PIECES, line)),
            dma((PIECES,)),
            dma((PIECES,)),
            dma((PIECES, 2)),
            dma((PIECES, 2)),
            dma((PIECES, 2)),
            dma((PIECES,)),
            dma((3,)),
            dma((ADAM_PARTS, 4)),
            dma((PIECES + 1,)),
        ],
        compiler_params=pltpu.CompilerParams(collective_id=0, has_side_effects=True, vmem_limit_bytes=40 << 20),
    )(
        *placed(pltpu.HBM, tokens, norm_gain, lengths, queries, key_cache, value_cache, master, moment_first, moment_second, gradient),
    )
    return pl.pallas_call(
        functools.partial(write_kernel, (few, steps, slots, share, kv_heads)),
        out_shape=tuple(jax.ShapeDtypeStruct(result.shape, result.dtype) for result in results[:5]),
        in_specs=[vmem] * len(results),
        out_specs=(anywhere,) * 5,
        scratch_shapes=[pltpu.VMEM((batch_rows // PIECES, steps, queries.shape[2]), jnp.bfloat16), dma((6,))],
        compiler_params=pltpu.CompilerParams(vmem_limit_bytes=8 << 20),
    )(*placed(pltpu.VMEM, *results))


def fits(sizes, tokens, master, queries, key_cache):
    grp, tp, fs = sizes
    batch_rows, steps, width = tokens.shape
    rows, depth, columns = batch_rows * steps, master.shape[0], master.shape[1]
    slots, kv_width = key_cache.shape[1:]
    if tp != 2 or fs != 2 or grp != 2 * tp * fs or width != 2 * depth or 128 % slots or slots % 16:
        return False
    few = 128 // slots
    return (
        depth % (32 * ADAM_PARTS) == 0 and depth % 128 == 0 and rows % 128 == 0 and rows % (16 * PIECES) == 0
        and columns == 2 * kv_width and few * steps % 16 == 0 and batch_rows % (few * PIECES) == 0
        and queries.shape[2] % kv_width == 0
    )


def project_gathered(tokens, norm_gain, layer_half):
    batch_rows, steps = (tokens.shape[0], tokens.shape[1])
    widened, gain_whole = (
        lax.all_gather(tokens, ("tp", "fs"), axis=2, tiled=True),
        lax.all_gather(norm_gain, ("tp", "fs"), axis=0, tiled=True),
    )
    mean_square = (
        jnp.einsum("rsd,rsd->rs", widened, widened, preferred_element_type=jnp.float32)[..., None]
        / MODEL_WIDTH
    )
    normed = (widened * lax.rsqrt(mean_square + norm_eps) * gain_whole.astype(jnp.float32)).astype(
        jnp.bfloat16
    )
    flattened = normed.reshape(batch_rows * steps, MODEL_WIDTH)
    gathered = lax.all_gather(layer_half, "grp", axis=0, tiled=True)
    return jnp.dot(flattened, gathered, preferred_element_type=jnp.float32)


def shards(
    sizes,
    tokens,
    norm_gain,
    queries,
    rotated_key_cache,
    head_value_cache,
    lengths,
    master,
    moment_first,
    moment_second,
    gradient,
):
    if fits(sizes, tokens, master, queries, rotated_key_cache):
        return project_and_attend(
            sizes, tokens, norm_gain, queries, rotated_key_cache, head_value_cache, lengths, master, moment_first, moment_second,
            gradient,
        )
    average = beta_first * moment_first + (1.0 - beta_first) * gradient
    variance = beta_second * moment_second + (1.0 - beta_second) * gradient * gradient
    update = average / correct_first / (jnp.sqrt(variance / correct_second) + adam_eps)
    renewed = master - learn_rate * (update + decay_rate * master)
    layer_half = renewed.astype(jnp.bfloat16)
    batch_rows, steps = (tokens.shape[0], tokens.shape[1])
    columns = layer_half.shape[1]
    projected_output = project_gathered(tokens, norm_gain, layer_half)
    kv_heads = columns // (2 * HEAD_SIZE)
    projected_output = projected_output.reshape(batch_rows, steps, kv_heads, 2, HEAD_SIZE)
    positions = (lengths[:, None] + jnp.arange(steps, dtype=jnp.int32)[None, :]).astype(jnp.float32)
    key_new = rotate(projected_output[:, :, :, 0, :], positions).astype(jnp.bfloat16)
    value_new = projected_output[:, :, :, 1, :].astype(jnp.bfloat16)
    appended = jnp.stack([key_new, value_new], axis=3).reshape(batch_rows, steps, columns)
    attended = attention(queries, rotated_key_cache, head_value_cache, key_new, value_new, lengths)
    return (attended, appended, renewed, average, variance)


def solution(mesh):
    in_specs = (
        P("grp", None, ("tp", "fs")),
        P(("tp", "fs")),
        P("grp", None, ("tp", "fs")),
        P("grp", None, ("tp", "fs")),
        P("grp", None, ("tp", "fs")),
        P("grp"),
        P("grp", ("tp", "fs")),
        P("grp", ("tp", "fs")),
        P("grp", ("tp", "fs")),
        P("grp", ("tp", "fs")),
    )
    out_specs = (
        P("grp", None, ("tp", "fs")),
        P("grp", None, ("tp", "fs")),
        P("grp", ("tp", "fs")),
        P("grp", ("tp", "fs")),
        P("grp", ("tp", "fs")),
    )
    return jax.shard_map(
        functools.partial(shards, tuple(mesh.shape[name] for name in ("grp", "tp", "fs"))), mesh=mesh, in_specs=in_specs, out_specs=out_specs, check_vma=False,
    )
```

```python
import functools
import math

import jax
import jax.numpy as jnp
from jax import lax
from jax.experimental import pallas as pl
from jax.experimental.pallas import tpu as pltpu
from jax.sharding import PartitionSpec as P

MESH_ID = pl.DeviceIdType.MESH
PIECES = 4
ADAM_PARTS = 8
AHEAD = 2
LEAD = 5
NEXT = 0
LAG = 3
LAG_GATE = 3

MODEL_WIDTH = 8192
QUERY_HEADS = 64
KEY_VALUE_HEADS = 8
HEAD_SIZE = 128


beta_first = 0.9
beta_second = 0.999
correct_first = 0.9999734386011124
correct_second = 0.09520785288629038
adam_eps = 1e-08
learn_rate = 0.003
decay_rate = 0.1
norm_eps = 1e-06
rope_base = 1000000.0


def rotate(keys, positions):
    halfway = keys.shape[-1] // 2
    frequency = rope_base ** (-(jnp.arange(halfway, dtype=jnp.float32) * 2.0 / keys.shape[-1]))
    angles = positions[:, :, None] * frequency[None, None, :]
    cosine = jnp.cos(angles)[:, :, None, :]
    sine = jnp.sin(angles)[:, :, None, :]
    first_half = keys[..., :halfway]
    second_half = keys[..., halfway:]
    return jnp.concatenate(
        [first_half * cosine - second_half * sine, second_half * cosine + first_half * sine],
        axis=-1,
    )


def attention(queries, rotated_key_cache, head_value_cache, key_new, value_new, lengths):
    batch_rows, steps = (queries.shape[0], queries.shape[1])
    window = rotated_key_cache.shape[1]
    kv_heads = rotated_key_cache.shape[2] // HEAD_SIZE
    sharing_factor = QUERY_HEADS // KEY_VALUE_HEADS
    factor = HEAD_SIZE ** (-0.5)
    query_heads = queries.reshape(batch_rows, steps, kv_heads, sharing_factor, HEAD_SIZE)
    cache_key_seeds = rotated_key_cache.reshape(batch_rows, window, kv_heads, HEAD_SIZE)
    cache_values = head_value_cache.reshape(batch_rows, window, kv_heads, HEAD_SIZE)
    scores_cached = (
        jnp.einsum(
            "rsxgd,rlxd->rxgsl", query_heads, cache_key_seeds, preferred_element_type=jnp.float32
        )
        * factor
    )
    scores_fresh = (
        jnp.einsum("rsxgd,ruxd->rxgsu", query_heads, key_new, preferred_element_type=jnp.float32)
        * factor
    )
    present = (jnp.arange(window, dtype=jnp.int32)[None, :] < lengths[:, None])[
        :, None, None, None, :
    ]
    causal = (
        jnp.arange(steps, dtype=jnp.int32)[None, :] <= jnp.arange(steps, dtype=jnp.int32)[:, None]
    )[None, None, None, :, :]
    scores_cached = jnp.where(present, scores_cached, -jnp.inf)
    scores_fresh = jnp.where(causal, scores_fresh, -jnp.inf)
    ceiling = jnp.maximum(
        jnp.max(scores_cached, axis=-1, keepdims=True),
        jnp.max(scores_fresh, axis=-1, keepdims=True),
    )
    probs_cached = jnp.exp(scores_cached - ceiling)
    probs_fresh = jnp.exp(scores_fresh - ceiling)
    denom = jnp.sum(probs_cached, axis=-1, keepdims=True) + jnp.sum(
        probs_fresh, axis=-1, keepdims=True
    )
    weights_cached = probs_cached.astype(jnp.bfloat16)
    weights_fresh = probs_fresh.astype(jnp.bfloat16)
    blended = jnp.einsum(
        "rxgsl,rlxd->rsxgd", weights_cached, cache_values, preferred_element_type=jnp.float32
    )
    blended = blended + jnp.einsum(
        "rxgsu,ruxd->rsxgd", weights_fresh, value_new, preferred_element_type=jnp.float32
    )
    blended = blended / jnp.transpose(denom, (0, 3, 1, 2, 4))
    return blended.astype(jnp.bfloat16).reshape(
        batch_rows, steps, kv_heads * sharing_factor * HEAD_SIZE
    )


def attend_new_rows(sizes, b, at, q_ref, app_ref, out_ref, part):
    few, steps, slots, share, kv_heads = sizes
    band = few * steps
    factor = HEAD_SIZE ** (-0.5)
    part_out, part_max, part_sum = part
    shape = (share * band, band)
    mine = lax.rem(lax.broadcasted_iota(jnp.int32, shape, 0), band)
    other_row = lax.broadcasted_iota(jnp.int32, shape, 1)
    valid = (mine // steps == other_row // steps) & (other_row <= mine)
    window = pl.ds(b * band, band)
    for x in range(kv_heads):
        lanes = [pl.ds((x * share + h) * HEAD_SIZE, HEAD_SIZE) for h in range(share)]
        keys = app_ref[window, pl.ds(2 * x * HEAD_SIZE, HEAD_SIZE)]
        values = app_ref[window, pl.ds((2 * x + 1) * HEAD_SIZE, HEAD_SIZE)]
        asked = jnp.concatenate([q_ref[pl.ds(b * few, few), :, cols].reshape(band, HEAD_SIZE) for cols in lanes], axis=0)
        scores = (
            lax.dot_general(asked, keys, (((1,), (1,)), ((), ())), preferred_element_type=jnp.float32) * factor
        )
        scores = jnp.where(valid, scores, -jnp.inf)
        before = part_max[x]
        most = jnp.maximum(before, jnp.max(scores, axis=1, keepdims=True))
        probs = jnp.exp(scores - most[:, :1])
        again = jnp.exp(before - most)
        denom = again * part_sum[x] + jnp.sum(probs, axis=1, keepdims=True)
        blended = again * part_out[x] + jnp.dot(probs.astype(jnp.bfloat16), values, preferred_element_type=jnp.float32)
        blended = (blended / denom).astype(jnp.bfloat16)
        for h in range(share):
            out_ref[pl.ds(at * few, few), :, lanes[h]] = blended[h * band : (h + 1) * band].reshape(few, steps, HEAD_SIZE)


def exchange_kernel(sizes, tok_hbm, gain_hbm, len_ref, q_hbm, k_hbm, v_hbm, mas_hbm, fir_hbm, sec_hbm, gra_hbm, out_ref,
                    new_ref, mas_ref, fir_ref, sec_ref, q_ref, app_ref, late_out, late_max, late_sum, tok_ref, gain_ref, cos_ref,
                    sin_ref, present_ref, gra_ref, w_ref,
                    sent, transit, held, squares, squares_in, scale_ref, total, pair_out, pair_in, near_out, near_in, mid_out,
                    mid_in, far_out, far_in, k_ref, v_ref, part_out, part_max, part_sum, sq_s, sq_r, tok_s, tok_r, tr_r,
                    rl_s, fx_s, fc_s, pair_s, pair_r, near_s, near_r, mid_s, mid_r, far_s, far_r, load_s, adam_s, first_s):
    grp, tp, fs = sizes
    line = grp // 2
    g, t, f = lax.axis_index("grp"), lax.axis_index("tp"), lax.axis_index("fs")
    z, y = g // 2, lax.rem(g, 2)
    batch_rows, steps, width = tok_ref.shape
    rows = batch_rows * steps
    depth = w_ref.shape[0]
    blocks = width // depth
    piece = rows // PIECES
    lot = batch_rows // PIECES
    me = t * fs + f
    owner_t, owner_f = z // fs, lax.rem(z, fs)
    half_z, side = z // 2, lax.rem(z, 2)
    near = half_z * 2 + 1 - side
    gate = side != half_z
    far_gate = 2 - half_z
    far_outer = 3 * (1 - half_z)
    zs_of = (z, near, far_gate, far_outer)

    def remote(src, dst, ss, rs, device):
        return pltpu.make_async_remote_copy(
            src_ref=src, dst_ref=dst, send_sem=ss, recv_sem=rs, device_id=device, device_id_type=MESH_ID
        )

    barrier = pltpu.get_barrier_semaphore()
    mates = [(g, 1 - t, f), (g, t, 1 - f), (g, 1 - t, 1 - f)]
    peers = [(lax.rem(g + i, grp), t, k) for i in range(1, grp) for k in (f, 1 - f)]
    loads = [
        pltpu.make_async_copy(src, dst, load_s.at[i])
        for i, (src, dst) in enumerate(((q_hbm, q_ref), (k_hbm, k_ref), (v_hbm, v_ref)))
    ]
    part_rows = depth // ADAM_PARTS
    adam_loads = [
        [
            pltpu.make_async_copy(src.at[pl.ds(a * part_rows, part_rows)], dst.at[pl.ds(a * part_rows, part_rows)], adam_s.at[a, i])
            for i, (src, dst) in enumerate(((mas_hbm, mas_ref), (fir_hbm, fir_ref), (sec_hbm, sec_ref), (gra_hbm, gra_ref)))
        ]
        for a in range(ADAM_PARTS)
    ]
    first = [pltpu.make_async_copy(gain_hbm, gain_ref, first_s.at[PIECES])] + [
        pltpu.make_async_copy(tok_hbm.at[pl.ds(c * lot, lot)], tok_ref.at[pl.ds(c * lot, lot)], first_s.at[c])
        for c in range(PIECES)
    ]
    for copy in first:
        copy.start()
    for device in peers + mates:
        pl.semaphore_signal(barrier, inc=1, device_id=device, device_id_type=MESH_ID)
    for copies in adam_loads:
        for copy in copies:
            copy.start()
    for copy in loads:
        copy.start()

    def tokens_of(c, cols):
        return tok_ref[pl.ds(c * lot, lot), :, cols].reshape(piece, cols.size).astype(jnp.float32)

    def fill(c):
        for copy in first[: 2] if c == 0 else first[c + 1 : c + 2]:
            copy.wait()
        for j in range(blocks):
            cols = pl.ds(j * depth, depth)
            gain = gain_ref[cols].astype(jnp.float32).reshape(1, depth)
            sent[c, j] = (tokens_of(c, cols) * gain).astype(jnp.bfloat16)

    def send(c, end):
        for turn in range(2):
            j = lax.rem(y + c + turn, 2)
            dest = me * blocks + j
            src = sent.at[c, j]
            away = remote(src, held.at[c, g], tok_s.at[c, turn], tok_r.at[c, g], (dest, t, f))
            cross = remote(src, transit.at[c], tok_s.at[c, turn], tr_r.at[c], mates[1])
            direct = (dest != g) if turn == 0 else (dest != g) & (me == z)

            @pl.when(direct)
            def _():
                away.wait_send() if end else away.start()

            if turn == 1:

                @pl.when(me != z)
                def _():
                    cross.wait_send() if end else cross.start()

            if not end:

                @pl.when(dest == g)
                def _():
                    pltpu.make_async_copy(src, held.at[c, g], tok_r.at[c, g]).start()

    other = t * fs + 1 - f

    def relay(c, end):
        j = lax.rem(y + c + 1, 2)
        copy = remote(transit.at[c], held.at[c, g], rl_s.at[c], tok_r.at[c, g], (other * blocks + j, t, f))

        @pl.when(other != z)
        def _():
            if end:
                copy.wait_send()
            else:
                remote(transit.at[c], transit.at[c], rl_s.at[c], tr_r.at[c], mates[1]).wait_recv()
                copy.start()

    def slot_copies(c, i, turn):
        slot = zs_of[i] * 2 + lax.rem(y + c + turn, 2)
        first_f = owner_f if i == 0 or turn == 0 else 1 - owner_f
        block = held.at[c, slot]
        across = remote(block, block, fx_s.at[c, 2 * i + turn], tok_r.at[c, slot], mates[1])
        beside = remote(block, block, fc_s.at[c, 2 * i + turn], tok_r.at[c, slot], mates[0])
        return across, beside, first_f

    def lead(c, i):
        for turn in range(2):
            across, beside, first_f = slot_copies(c, i, turn)

            @pl.when((t == owner_t) & (f == first_f))
            def _():
                across.wait_recv()
                across.start()
                beside.start()

    def second(c, i):
        for turn in range(2):
            across, beside, first_f = slot_copies(c, i, turn)

            @pl.when((t == owner_t) & (f != first_f))
            def _():
                across.wait_recv()
                beside.start()

    def third(c, i):
        for turn in range(2):
            across, _, _ = slot_copies(c, i, turn)

            @pl.when(t != owner_t)
            def _():
                across.wait_recv()

    def sent_on(c, i):
        for turn in range(2):
            across, beside, first_f = slot_copies(c, i, turn)

            @pl.when((t == owner_t) & (f == first_f))
            def _():
                across.wait_send()

            @pl.when(t == owner_t)
            def _():
                beside.wait_send()

    def adam(a):
        for copy in adam_loads[a]:
            copy.wait()
        few_rows = 32

        def body(r, carry):
            window = pl.ds(pl.multiple_of(a * part_rows + r * few_rows, few_rows), few_rows)
            slope, old = gra_ref[window, :], mas_ref[window, :]
            average = beta_first * fir_ref[window, :] + (1.0 - beta_first) * slope
            variance = beta_second * sec_ref[window, :] + (1.0 - beta_second) * slope * slope
            update = average / correct_first / (jnp.sqrt(variance / correct_second) + adam_eps)
            renewed = old - learn_rate * (update + decay_rate * old)
            fir_ref[window, :] = average
            sec_ref[window, :] = variance
            mas_ref[window, :] = renewed
            w_ref[window, :] = renewed.astype(jnp.bfloat16)
            return carry

        lax.fori_loop(0, part_rows // few_rows, body, 0)

    sq = [remote(squares, squares_in.at[i], sq_s.at[i], sq_r.at[i], mates[i]) for i in range(3)]

    def start_squares():
        for c in range(PIECES):
            wide = tokens_of(c, pl.ds(0, width))
            wide = wide * wide
            part = wide[:, :128]
            for i in range(1, width // 128):
                part = part + wide[:, i * 128 : (i + 1) * 128]
            scale_ref[pl.ds(c * piece, piece), :] = part
        squares[...] = jnp.broadcast_to(jnp.sum(scale_ref[...].T, axis=0, keepdims=True), squares.shape)
        for copy in sq:
            copy.start()

    def finish_squares():
        for copy in sq:
            copy.wait()
        summed = (squares[...] + squares_in[0]) + (squares_in[1] + squares_in[2])
        scale = lax.rsqrt(summed / (width * tp * fs) + norm_eps)
        scale_ref[...] = jnp.broadcast_to(scale[0:1], (128, rows)).T

    def pair_copy(c, i):
        return remote(pair_out.at[c, i], pair_in.at[c, i], pair_s.at[c, i], pair_r.at[c, i], (z * 2 + 1 - y, t, f))

    def near_copy(c):
        return remote(near_out.at[c], near_in.at[c], near_s.at[c], near_r.at[c], (near * 2 + y, t, f))

    def mid_copy(c, k):
        return remote(mid_out.at[c, k], mid_in.at[c, k], mid_s.at[c, k], mid_r.at[c, k], (near * 2 + y, t, f))

    def far_copy(c, k):
        return remote(far_out.at[c, k], far_in.at[c], far_s.at[c, k], far_r.at[c], (zs_of[2 + k] * 2 + y, t, f))

    def multiply(c, i):
        slots2 = held[c, pl.ds(zs_of[i] * 2, 2)].reshape(2 * piece, depth)
        product = jnp.dot(slots2, w_ref[...], preferred_element_type=jnp.float32)
        total[c, i] = product.reshape(2, piece, product.shape[1])
        pair_out[c, i] = total[c, i, 1 - y].astype(jnp.bfloat16)
        pair_copy(c, i).start()

    def combine(c, i):
        pair_copy(c, i).wait_recv()
        both = total[c, i, y] + pair_in[c, i].astype(jnp.float32)
        if i == 0:
            total[c, 0, 0] = both
        elif i == 1:
            near_out[c] = both.astype(jnp.bfloat16)
            near_copy(c).start()
        else:

            @pl.when(gate)
            def _():
                total[c, i, 0] = both

            @pl.when(jnp.logical_not(gate))
            def _():
                mid_out[c, i - 2] = both.astype(jnp.bfloat16)
                mid_copy(c, i - 2).start()

    def pass_on(c, i):
        if i >= 2:

            @pl.when(gate)
            def _():
                mid_copy(c, i - 2).wait_recv()
                far_out[c, i - 2] = (total[c, i, 0] + mid_in[c, i - 2].astype(jnp.float32)).astype(jnp.bfloat16)
                far_copy(c, i - 2).start()

    _, slots, kv_width = k_ref.shape
    kv_heads = kv_width // HEAD_SIZE
    share = q_ref.shape[2] // kv_width
    few = 128 // slots
    band = few * steps
    factor = HEAD_SIZE ** (-0.5)
    chunks = batch_rows // few
    over_last = (((1,), (1,)), ((), ()))

    def head_lanes(x, h):
        return pl.ds((x * share + h) * HEAD_SIZE, HEAD_SIZE)

    def some_queries(b, x):
        return jnp.concatenate(
            [q_ref[pl.ds(b * few, few), :, head_lanes(x, h)].reshape(band, HEAD_SIZE) for h in range(share)], axis=0
        )

    early = chunks - chunks // PIECES

    def parts_of(b):
        if b < early:
            return part_out.at[b], part_max.at[b], part_sum.at[b]
        return late_out.at[b - early], late_max.at[b - early], late_sum.at[b - early]

    def attend_cached(b):
        to_out, to_max, to_sum = parts_of(b)
        shape = (share * band, few * slots)
        row = lax.rem(lax.broadcasted_iota(jnp.int32, shape, 0), band) // steps
        same = row == lax.broadcasted_iota(jnp.int32, shape, 1) // slots
        valid = same & (present_ref[pl.ds(b, 1), :] > 0.5)
        for x in range(kv_heads):
            lanes = pl.ds(x * HEAD_SIZE, HEAD_SIZE)
            keys = k_ref[pl.ds(b * few, few), :, lanes].reshape(few * slots, HEAD_SIZE)
            values = v_ref[pl.ds(b * few, few), :, lanes].reshape(few * slots, HEAD_SIZE)
            scores = (
                lax.dot_general(some_queries(b, x), keys, over_last, preferred_element_type=jnp.float32) * factor
            )
            scores = jnp.where(valid, scores, -jnp.inf)
            most = jnp.max(scores, axis=1, keepdims=True)
            probs = jnp.exp(scores - most)
            to_max[x] = jnp.broadcast_to(most, (share * band, HEAD_SIZE))
            to_sum[x] = jnp.broadcast_to(jnp.sum(probs, axis=1, keepdims=True), (share * band, HEAD_SIZE))
            to_out[x] = jnp.dot(probs.astype(jnp.bfloat16), values, preferred_element_type=jnp.float32)

    def attend_new(b):
        attend_new_rows((few, steps, slots, share, kv_heads), b, b, q_ref, app_ref, out_ref, parts_of(b))

    half = HEAD_SIZE // 2

    def prepare():
        lane = lax.broadcasted_iota(jnp.int32, (1, few * slots), 1)
        for b in range(chunks):
            lengths = jnp.full(lane.shape, len_ref[b * few], jnp.int32)
            for k in range(1, few):
                lengths = jnp.where(lane // slots == k, len_ref[b * few + k], lengths)
            present_ref[pl.ds(b, 1), :] = (lax.rem(lane, slots) < lengths).astype(jnp.float32)
        for b in range(batch_rows):
            cos_ref[pl.ds(b * steps, steps), :] = jnp.full((steps, HEAD_SIZE), len_ref[b].astype(jnp.float32))
        lane = lax.broadcasted_iota(jnp.int32, (8, HEAD_SIZE), 1)
        exponent = lax.rem(lane, half).astype(jnp.float32) * (2.0 / HEAD_SIZE)
        frequency = jnp.exp(exponent * (-math.log(rope_base)))
        sign = jnp.where(lane < half, -1.0, 1.0)
        step = lax.rem(lax.broadcasted_iota(jnp.int32, (8, HEAD_SIZE), 0), steps).astype(jnp.float32)

        def body(r, carry):
            window = pl.ds(pl.multiple_of(r * 8, 8), 8)
            angles = (cos_ref[window, :] + step) * frequency
            cos_ref[window, :] = jnp.cos(angles)
            sin_ref[window, :] = jnp.sin(angles) * sign
            return carry

        lax.fori_loop(0, rows // 8, body, 0)

    def finish(c):
        window = pl.ds(c * piece, piece)
        near_copy(c).wait_recv()
        far_copy(c, 0).wait_recv()
        scale = scale_ref[window, :]
        for x in range(kv_heads):
            lanes = pl.ds(2 * x * HEAD_SIZE, HEAD_SIZE)
            later = pl.ds((2 * x + 1) * HEAD_SIZE, HEAD_SIZE)

            def summed(cols):
                arrived = near_in[c, :, cols].astype(jnp.float32) + far_in[c, :, cols].astype(jnp.float32)
                return (total[c, 0, 0, :, cols] + arrived) * scale

            key = summed(lanes)
            key = key * cos_ref[window, :] + pltpu.roll(key, half, 1) * sin_ref[window, :]
            for cols, part in ((lanes, key), (later, summed(later))):
                part = part.astype(jnp.bfloat16)
                app_ref[window, cols] = part
                new_ref[pl.ds(c * lot, lot), :, cols] = part.reshape(lot, steps, HEAD_SIZE)
        for b in range(c * chunks // PIECES, min((c + 1) * chunks // PIECES, early)):
            attend_new(b)

    fill(0)
    pl.semaphore_wait(barrier, len(peers) + len(mates))
    send(0, False)
    for c in range(1, AHEAD):
        fill(c)
        send(c, False)
    for c in range(AHEAD, PIECES):
        fill(c)
    start_squares()
    prepare()

    order = [(c, i) for c in range(PIECES) for i in ((0, 1, 2, 3) if c == 0 else (3, 2, 1, 0))]
    count = len(order)

    def arrive(n):
        c, i = order[n]
        if n % line == 0:
            if c == 0:
                relay(0, False)
            if c + AHEAD < PIECES:
                send(c + AHEAD, False)
            if c + 1 < PIECES:
                relay(c + 1, False)
        lead(c, i)

    for n in range(LEAD):
        adam_until = (n + 1) * ADAM_PARTS // LEAD
        for a in range(n * ADAM_PARTS // LEAD, adam_until):
            adam(a)
        arrive(n)
        if n >= LEAD - NEXT:
            second(*order[n - LEAD + NEXT])
    finish_squares()
    for copy in loads:
        copy.wait()
    done = 0
    steps_now = -(-chunks // (count - 4))
    def drain(c):
        send(c, True)
        relay(c, True)
        for i in range(line):
            sent_on(c, i)
            pair_copy(c, i).wait_send()
        near_copy(c).wait_send()
        for k in range(2):

            @pl.when(gate)
            def _():
                far_copy(c, k).wait_send()

            @pl.when(jnp.logical_not(gate))
            def _():
                mid_copy(c, k).wait_send()

    def combine_range(start, stop):
        for m in range(max(start, 0), stop):
            combine(*order[m])

    def pass_range(start, stop):
        for m in range(max(start, 0), stop):
            pass_on(*order[m])
            if m % line == line - 1 and line <= m < count - 1:
                finish(m // line - 1)
                drain(m // line - 1)

    for n in range(count):
        if n + LEAD < count:
            arrive(n + LEAD)
        if n + NEXT < count:
            second(*order[n + NEXT])
        third(*order[n])
        multiply(*order[n])
        combine_range(n - LAG, n - LAG + 1)
        for b in range(done, min(done + steps_now, chunks)):
            attend_cached(b)
        done = min(done + steps_now, chunks)
        pass_range(n - LAG - LAG_GATE, n - LAG - LAG_GATE + 1)
    last = count - line
    combine_range(count - LAG, last + 3)
    pass_range(count - LAG - LAG_GATE, last + 2)
    combine_range(max(count - LAG, last + 3), count)
    finish(PIECES - 2)
    drain(PIECES - 2)
    finish(PIECES - 1)
    drain(PIECES - 1)


def write_kernel(sizes, att_ref, new_ref, mas_ref, fir_ref, sec_ref, q_ref, app_ref, late_out, late_max, late_sum, att_hbm,
                 new_hbm, mas_hbm, fir_hbm, sec_hbm, tail_ref, write_s):
    few = sizes[0]
    late = late_out.shape[0]
    early = att_ref.shape[0] // few - late
    first = pl.ds(0, early * few)
    moves = ((mas_ref, mas_hbm), (fir_ref, fir_hbm), (sec_ref, sec_hbm), (new_ref, new_hbm), (att_ref.at[first], att_hbm.at[first]))
    copies = [pltpu.make_async_copy(src, dst, write_s.at[i]) for i, (src, dst) in enumerate(moves)]
    for copy in copies:
        copy.start()
    for b in range(late):
        attend_new_rows(
            sizes, early + b, b, q_ref, app_ref, tail_ref, (late_out.at[b], late_max.at[b], late_sum.at[b])
        )
    copies.append(pltpu.make_async_copy(tail_ref, att_hbm.at[pl.ds(early * few, late * few)], write_s.at[len(moves)]))
    copies[-1].start()
    for copy in copies:
        copy.wait()


def project_and_attend(sizes, tokens, norm_gain, queries, key_cache, value_cache, lengths, master, moment_first, moment_second,
                       gradient):
    grp, _, _ = sizes
    batch_rows, steps, width = tokens.shape
    _, slots, kv_width = key_cache.shape
    rows = batch_rows * steps
    depth, columns = master.shape
    blocks, line = width // depth, grp // 2
    kv_heads, share = kv_width // HEAD_SIZE, queries.shape[2] // kv_width
    few = 128 // slots
    piece = rows // PIECES
    dma = pltpu.SemaphoreType.DMA
    vmem = pl.BlockSpec(memory_space=pltpu.VMEM)
    anywhere = pl.BlockSpec(memory_space=pltpu.HBM)
    smem = pl.BlockSpec(memory_space=pltpu.SMEM)
    chunks, block = batch_rows // few, (kv_heads, share * few * steps, HEAD_SIZE)
    late = pltpu.VMEM((chunks // PIECES, *block), jnp.float32)
    part = pltpu.VMEM((chunks - chunks // PIECES, *block), jnp.float32)
    state = pltpu.VMEM(master.shape, jnp.float32)

    def placed(space, *arrays):
        return [pltpu.with_memory_space_constraint(array, space) for array in arrays]

    def half_width(*lead):
        return pltpu.VMEM((PIECES, *lead, piece, columns), jnp.bfloat16)

    results = pl.pallas_call(
        functools.partial(exchange_kernel, sizes),
        out_shape=(
            pltpu.VMEM(queries.shape, jnp.bfloat16),
            pltpu.VMEM((batch_rows, steps, columns), jnp.bfloat16),
            state,
            state,
            state,
            pltpu.VMEM(queries.shape, jnp.bfloat16),
            pltpu.VMEM((rows, columns), jnp.bfloat16),
            late,
            late,
            late,
        ),
        in_specs=[anywhere] * 2 + [smem] + [anywhere] * 7,
        out_specs=(vmem,) * 10,
        scratch_shapes=[
            pltpu.VMEM(tokens.shape, jnp.bfloat16),
            pltpu.VMEM((width,), jnp.bfloat16),
            pltpu.VMEM((rows, HEAD_SIZE), jnp.float32),
            pltpu.VMEM((rows, HEAD_SIZE), jnp.float32),
            pltpu.VMEM((batch_rows // few, few * slots), jnp.float32),
            pltpu.VMEM(master.shape, jnp.float32),
            pltpu.VMEM(master.shape, jnp.bfloat16),
            pltpu.VMEM((PIECES, blocks, piece, depth), jnp.bfloat16),
            pltpu.VMEM((PIECES, piece, depth), jnp.bfloat16),
            pltpu.VMEM((PIECES, grp, piece, depth), jnp.bfloat16),
            pltpu.VMEM((8, rows), jnp.float32),
            pltpu.VMEM((3, 8, rows), jnp.float32),
            pltpu.VMEM((rows, 128), jnp.float32),
            pltpu.VMEM((PIECES, line, 2, piece, columns), jnp.float32),
            half_width(line),
            half_width(line),
            half_width(),
            half_width(),
            half_width(2),
            half_width(2),
            half_width(2),
            half_width(),
            pltpu.VMEM(key_cache.shape, jnp.bfloat16),
            pltpu.VMEM(value_cache.shape, jnp.bfloat16),
            part,
            part,
            part,
            dma((3,)),
            dma((3,)),
            dma((PIECES, 2)),
            dma((PIECES, grp)),
            dma((PIECES,)),
            dma((PIECES,)),
            dma((PIECES, grp)),
            dma((PIECES, grp)),
            dma((PIECES, line)),
            dma((PIECES, line)),
            dma((PIECES,)),
            dma((PIECES,)),
            dma((PIECES, 2)),
            dma((PIECES, 2)),
            dma((PIECES, 2)),
            dma((PIECES,)),
            dma((3,)),
            dma((ADAM_PARTS, 4)),
            dma((PIECES + 1,)),
        ],
        compiler_params=pltpu.CompilerParams(collective_id=0, has_side_effects=True, vmem_limit_bytes=40 << 20),
    )(
        *placed(pltpu.HBM, tokens, norm_gain, lengths, queries, key_cache, value_cache, master, moment_first, moment_second, gradient),
    )
    return pl.pallas_call(
        functools.partial(write_kernel, (few, steps, slots, share, kv_heads)),
        out_shape=tuple(jax.ShapeDtypeStruct(result.shape, result.dtype) for result in results[:5]),
        in_specs=[vmem] * len(results),
        out_specs=(anywhere,) * 5,
        scratch_shapes=[pltpu.VMEM((batch_rows // PIECES, steps, queries.shape[2]), jnp.bfloat16), dma((6,))],
        compiler_params=pltpu.CompilerParams(vmem_limit_bytes=8 << 20),
    )(*placed(pltpu.VMEM, *results))


def fits(sizes, tokens, master, queries, key_cache):
    grp, tp, fs = sizes
    batch_rows, steps, width = tokens.shape
    rows, depth, columns = batch_rows * steps, master.shape[0], master.shape[1]
    slots, kv_width = key_cache.shape[1:]
    if tp != 2 or fs != 2 or grp != 2 * tp * fs or width != 2 * depth or 128 % slots or slots % 16:
        return False
    few = 128 // slots
    return (
        depth % (32 * ADAM_PARTS) == 0 and depth % 128 == 0 and rows % 128 == 0 and rows % (16 * PIECES) == 0
        and columns == 2 * kv_width and few * steps % 16 == 0 and batch_rows % (few * PIECES) == 0
        and queries.shape[2] % kv_width == 0
    )


def project_gathered(tokens, norm_gain, layer_half):
    batch_rows, steps = (tokens.shape[0], tokens.shape[1])
    widened, gain_whole = (
        lax.all_gather(tokens, ("tp", "fs"), axis=2, tiled=True),
        lax.all_gather(norm_gain, ("tp", "fs"), axis=0, tiled=True),
    )
    mean_square = (
        jnp.einsum("rsd,rsd->rs", widened, widened, preferred_element_type=jnp.float32)[..., None]
        / MODEL_WIDTH
    )
    normed = (widened * lax.rsqrt(mean_square + norm_eps) * gain_whole.astype(jnp.float32)).astype(
        jnp.bfloat16
    )
    flattened = normed.reshape(batch_rows * steps, MODEL_WIDTH)
    gathered = lax.all_gather(layer_half, "grp", axis=0, tiled=True)
    return jnp.dot(flattened, gathered, preferred_element_type=jnp.float32)


def shards(
    sizes,
    tokens,
    norm_gain,
    queries,
    rotated_key_cache,
    head_value_cache,
    lengths,
    master,
    moment_first,
    moment_second,
    gradient,
):
    if fits(sizes, tokens, master, queries, rotated_key_cache):
        return project_and_attend(
            sizes, tokens, norm_gain, queries, rotated_key_cache, head_value_cache, lengths, master, moment_first, moment_second,
            gradient,
        )
    average = beta_first * moment_first + (1.0 - beta_first) * gradient
    variance = beta_second * moment_second + (1.0 - beta_second) * gradient * gradient
    update = average / correct_first / (jnp.sqrt(variance / correct_second) + adam_eps)
    renewed = master - learn_rate * (update + decay_rate * master)
    layer_half = renewed.astype(jnp.bfloat16)
    batch_rows, steps = (tokens.shape[0], tokens.shape[1])
    columns = layer_half.shape[1]
    projected_output = project_gathered(tokens, norm_gain, layer_half)
    kv_heads = columns // (2 * HEAD_SIZE)
    projected_output = projected_output.reshape(batch_rows, steps, kv_heads, 2, HEAD_SIZE)
    positions = (lengths[:, None] + jnp.arange(steps, dtype=jnp.int32)[None, :]).astype(jnp.float32)
    key_new = rotate(projected_output[:, :, :, 0, :], positions).astype(jnp.bfloat16)
    value_new = projected_output[:, :, :, 1, :].astype(jnp.bfloat16)
    appended = jnp.stack([key_new, value_new], axis=3).reshape(batch_rows, steps, columns)
    attended = attention(queries, rotated_key_cache, head_value_cache, key_new, value_new, lengths)
    return (attended, appended, renewed, average, variance)


def solution(mesh):
    in_specs = (
        P("grp", None, ("tp", "fs")),
        P(("tp", "fs")),
        P("grp", None, ("tp", "fs")),
        P("grp", None, ("tp", "fs")),
        P("grp", None, ("tp", "fs")),
        P("grp"),
        P("grp", ("tp", "fs")),
        P("grp", ("tp", "fs")),
        P("grp", ("tp", "fs")),
        P("grp", ("tp", "fs")),
    )
    out_specs = (
        P("grp", None, ("tp", "fs")),
        P("grp", None, ("tp", "fs")),
        P("grp", ("tp", "fs")),
        P("grp", ("tp", "fs")),
        P("grp", ("tp", "fs")),
    )
    return jax.shard_map(
        functools.partial(shards, tuple(mesh.shape[name] for name in ("grp", "tp", "fs"))), mesh=mesh, in_specs=in_specs, out_specs=out_specs, check_vma=False,
    )
```
